32 devices in a mesh: row: 2 (over y), col: 16 (over z, x, core).
Axes of the slice: x: 2, y: 2, z: 4, core: 2. Of those that a mesh axis runs over, the one named last changes fastest.
Arguments:
- queries: bfloat16 [8192, 1024], P(('row', 'col')), may hold values from -8 to 8
- key_rows: bfloat16 [8192, 1024], P(('row', 'col')), may hold values from -8 to 8
- value_rows: bfloat16 [8192, 1024], P(('row', 'col')), may hold values from -6 to 6
- out_grad: bfloat16 [8192, 1024], P(('row', 'col')), may hold values from -6 to 6
- dropout_bits: int32 [8192, 128], P(('row', 'col')), may hold values from 0 to 255, as said below
- partner: int32 [3, 2, 16], replicated, may hold values from 0 to 15, each once within a row
- block_pick: int32 [3, 2, 16], replicated, may hold values from 0 to 1
- global_blocks: int32 [2], replicated, may hold values from 0 to 63
Outputs:
- attended: bfloat16 [8192, 1024], P(('row', 'col'))
- query_grad: bfloat16 [8192, 1024], P(('row', 'col'))
- key_grad: bfloat16 [8192, 1024], P(('row', 'col'))
- value_grad: bfloat16 [8192, 1024], P(('row', 'col'))
The draws below stay inside these ranges and needn't reach their ends.
Inputs may be any that keep to these rules, and one draw needn't show every extreme that they name: `dropout_bits`: each word packs 8 flags of 0 or 1 in its low bits. partner[r, a, :] is a permutation of the places 0 to 15.
All inputs are finite; a program needn't handle non-finite values.
Results may differ from the reference program's by a relative error of at most 0.0085.
Values may be sent and summed in bfloat16 or wider, within the bound.
A program may use at most 128 MiB of HBM per device.

```python
import jax
import jax.numpy as jnp
from jax import lax

HEADS = 16
HEAD_DIM = 64
BLOCK = 128
NGLOBAL = 2
NMATCH = 3
TOK_DEV = 256
WIDTH = 1024
BANDS = 2
PEERS = 16
TOKENS = 8192
NBLOCKS = 64
BLK_DEV = 2
SLOTS = 8
WORDS = 128


def draw_queries(key, part):
    base = jnp.clip(jax.random.normal(jax.random.fold_in(key, 1), (TOKENS, WIDTH), jnp.float32), -4.0, 4.0)
    return base.astype(jnp.bfloat16)


def draw_key_rows(key, part):
    base = jnp.clip(jax.random.normal(jax.random.fold_in(key, 2), (TOKENS, WIDTH), jnp.float32), -4.0, 4.0)
    return base.astype(jnp.bfloat16)


def draw_dropout_bits(key, part):
    rolls = jax.random.randint(jax.random.fold_in(key, 3), (TOKENS, WORDS, 8), 0, 10)
    kept = (rolls != 0).astype(jnp.int32)
    weights = jnp.left_shift(jnp.ones((8,), jnp.int32), jnp.arange(8, dtype=jnp.int32))
    return jnp.sum(kept * weights, -1).astype(jnp.int32)


def place_ends(values, stream_key, low, top_value):
    shape = values.shape
    index_at = [jax.random.randint(jax.random.fold_in(stream_key, axis), (), 0, shape[axis]) for axis in range(len(shape))]
    values = values.at[tuple(index_at)].set(low)
    longest = shape.index(max(shape))
    index_at[longest] = (index_at[longest] + 1) % shape[longest]
    return values.at[tuple(index_at)].set(top_value)


def block_scale(stream_key, dims, pieces, least, largest):
    gain, own = 1.0, jax.random.fold_in(stream_key, 6)
    for dim, shards_of in pieces:
        steps = jnp.exp(jax.random.uniform(jax.random.fold_in(own, dim), (shards_of,), jnp.float32, least / len(pieces), largest / len(pieces)))
        gain = gain * jnp.repeat(steps, dims[dim] // shards_of).reshape([-1 if axis == dim else 1 for axis in range(len(dims))])
    return gain


def gaussian(stream_key, dims, deviation, reach, pieces=(), kind=jnp.bfloat16):
    array = deviation * jax.random.normal(stream_key, dims, jnp.float32)
    if pieces:
        array = array * block_scale(stream_key, dims, pieces, -0.22, 0.18)
    return jnp.clip(array, -reach, reach).astype(kind)


def setup_inputs(seed: int = 0) -> dict:
    key_of = jax.random.split(jax.random.key(seed), 9)
    return {
        "queries": draw_queries(jax.random.fold_in(key_of[8], 71), 0),
        "key_rows": draw_key_rows(jax.random.fold_in(key_of[8], 71), 0),
        "value_rows": gaussian(key_of[2], (TOKENS, WIDTH), 1.0, 6.0, ((0, 32),)),
        "out_grad": gaussian(key_of[3], (TOKENS, WIDTH), 1.0, 6.0, ((0, 32),)),
        "dropout_bits": draw_dropout_bits(jax.random.fold_in(key_of[8], 71), 0),
        "partner": jax.vmap(lambda own: jax.random.permutation(own, PEERS))(jax.random.split(key_of[5], NMATCH * BANDS)).reshape((NMATCH, BANDS, PEERS)).astype(jnp.int32),
        "block_pick": place_ends(jax.random.randint(key_of[6], (NMATCH, BANDS, PEERS), 0, BLK_DEV), jax.random.fold_in(key_of[6], 1), 0, BLK_DEV - 1).astype(jnp.int32),
        "global_blocks": jax.random.randint(key_of[7], (NGLOBAL,), 0, NBLOCKS).astype(jnp.int32),
    }


score_scale = 0.125
keep_scale = 1.0 / 0.9


def unpack_bits(packed):
    shifts = jnp.arange(8, dtype=jnp.int32)
    flags = jnp.right_shift(packed[..., None], shifts) & 1
    return flags.reshape(packed.shape[:-1] + (packed.shape[-1] * 8,))


def round_trip(values):
    return lax.optimization_barrier(values.astype(jnp.bfloat16)).astype(jnp.float32)


def reference(queries, key_rows, value_rows, out_grad, dropout_bits, partner, block_pick, global_blocks):
    width_all = HEADS * HEAD_DIM
    both_rows = jnp.concatenate([key_rows, value_rows], 1).reshape(NBLOCKS, BLOCK, 2 * width_all)

    def segment_step(totals, segment):
        band_index = segment // PEERS
        place_index = segment % PEERS
        first = (segment * BLK_DEV).astype(jnp.int32)
        own_blocks = first + jnp.arange(BLK_DEV, dtype=jnp.int32)
        window_ids = jnp.stack([(own_blocks - 1) % NBLOCKS, own_blocks, (own_blocks + 1) % NBLOCKS], 1)
        random_ids = (band_index * PEERS + partner[:, band_index, place_index]) * BLK_DEV + block_pick[:, band_index, place_index]
        shared_ids = jnp.concatenate([global_blocks, random_ids]).astype(jnp.int32)
        slot_ids = jnp.concatenate([window_ids, jnp.broadcast_to(shared_ids[None, :], (BLK_DEV, NGLOBAL + NMATCH))], 1).astype(jnp.int32)
        gathered = both_rows[slot_ids].astype(jnp.float32).reshape(BLK_DEV, SLOTS * BLOCK, 2 * width_all)
        keys_f = gathered[..., :width_all].reshape(BLK_DEV, SLOTS * BLOCK, HEADS, HEAD_DIM)
        values_f = gathered[..., width_all:].reshape(BLK_DEV, SLOTS * BLOCK, HEADS, HEAD_DIM)
        start_row = (first * BLOCK).astype(jnp.int32)
        query_f = lax.dynamic_slice_in_dim(queries, start_row, TOK_DEV, 0).astype(jnp.float32).reshape(BLK_DEV, BLOCK, HEADS, HEAD_DIM)
        grad_f = lax.dynamic_slice_in_dim(out_grad, start_row, TOK_DEV, 0).astype(jnp.float32).reshape(BLK_DEV, BLOCK, HEADS, HEAD_DIM)
        words = lax.dynamic_slice_in_dim(dropout_bits, start_row, TOK_DEV, 0)
        keep_mask = (unpack_bits(words).astype(jnp.float32) * keep_scale).reshape(BLK_DEV, BLOCK, SLOTS * BLOCK)
        score = jnp.einsum('jqhd,jkhd->jhqk', query_f, keys_f) * score_scale
        top = jnp.max(score, -1, keepdims=True)
        log_total = top + jnp.log(jnp.sum(jnp.exp(score - top), -1, keepdims=True))
        probs = jnp.exp(score - log_total)
        dropped_f = round_trip(probs * keep_mask[:, None])
        attended = jnp.einsum('jhqk,jkhd->jqhd', dropped_f, values_f).astype(jnp.bfloat16).reshape(TOK_DEV, width_all)
        grad_p = jnp.einsum('jqhd,jkhd->jhqk', grad_f, values_f) * keep_mask[:, None]
        delta = jnp.sum(probs * grad_p, -1, keepdims=True)
        dscore = round_trip(probs * (grad_p - delta))
        query_grad = (score_scale * jnp.einsum('jhqk,jkhd->jqhd', dscore, keys_f)).astype(jnp.bfloat16).reshape(TOK_DEV, width_all)
        key_part = (score_scale * jnp.einsum('jhqk,jqhd->jkhd', dscore, query_f)).reshape(BLK_DEV, SLOTS, BLOCK, width_all)
        value_part = jnp.einsum('jhqk,jqhd->jkhd', dropped_f, grad_f).reshape(BLK_DEV, SLOTS, BLOCK, width_all)
        parts = jnp.concatenate([key_part, value_part], -1)
        nearby = jnp.zeros((BLK_DEV + 2, BLOCK, 2 * width_all), jnp.float32)
        for offset_slot in range(3):
            nearby = nearby.at[offset_slot:offset_slot + BLK_DEV].add(parts[:, offset_slot])
        totals = totals.at[own_blocks].add(nearby[1:BLK_DEV + 1])
        totals = totals.at[(first - 1) % NBLOCKS].add(round_trip(nearby[0]))
        totals = totals.at[(first + BLK_DEV) % NBLOCKS].add(round_trip(nearby[BLK_DEV + 1]))
        distant = jnp.sum(parts[:, 3:], 0)
        for global_slot in range(NGLOBAL):
            totals = totals.at[global_blocks[global_slot]].add(distant[global_slot])
        for matching in range(NMATCH):
            totals = totals.at[random_ids[matching]].add(round_trip(distant[NGLOBAL + matching]))
        return totals, (attended, query_grad)

    start_totals = jnp.zeros((NBLOCKS, BLOCK, 2 * width_all), jnp.float32)
    totals, (attended, query_grad) = lax.scan(segment_step, start_totals, jnp.arange(BANDS * PEERS, dtype=jnp.int32))
    totals = totals.reshape(TOKENS, 2 * width_all)
    return (attended.reshape(TOKENS, width_all), query_grad.reshape(TOKENS, width_all),
            totals[:, :width_all].astype(jnp.bfloat16), totals[:, width_all:].astype(jnp.bfloat16))
```

```python
import functools

import jax
import jax.numpy as jnp
from jax import lax
from jax.experimental import pallas as pl
from jax.experimental.pallas import tpu as pltpu
from jax.sharding import PartitionSpec as P

HEAD_DIM = 64
BLOCK = 128
NGLOBAL = 2
NMATCH = 3
PAIR = 2 * HEAD_DIM
SLOTS = 3 + NGLOBAL + NMATCH

score_scale = 0.125
keep_scale = 1.0 / 0.9


def contract(a, b, dim_a, dim_b):
    return lax.dot_general(a, b, (((dim_a,), (dim_b,)), ((), ())), preferred_element_type=jnp.float32)


def stride_of(count):
    return max(1, count // 2 - 1)


def fused_kernel(
    rows, cols, heads, blocks,
    q_ref, k_ref, v_ref, g_ref, bits_ref, partner_ref, pick_ref, global_ref,
    qa_land, kvg_land,
    kv_pack, qg_pack, kv_in, qg_in, bits_all, kv_ext, kv_turned, halo, shared, shared_turned,
    shared_keys, words_ref, s_ref, dsp_ref, acc_ref, rand_ref, gacc_ref, halo_acc, gacc_in, qa_out, kvg_out, inverse_ref,
    kv_send, kv_recv, qg_send, qg_recv, bit_send, bit_recv, row_send, row_recv, back_send, back_recv, qa_send, qa_recv, kvg_send, kvg_recv,
):
    me, band = lax.axis_index("col"), lax.axis_index("row")
    head, group = me % heads, me // heads
    levels = heads.bit_length() - 1
    last = cols * blocks
    first = lax.broadcasted_iota(jnp.int32, (BLOCK, PAIR), 1) < HEAD_DIM
    zero = jnp.zeros((BLOCK, PAIR), jnp.bfloat16)

    barrier = pltpu.get_barrier_semaphore()

    def hello(step, carry):
        pl.semaphore_signal(barrier, inc=1, device_id={"col": (me + step) % cols})
        return carry

    lax.fori_loop(1, cols, hello, 0)
    for step in range(1, rows):
        pl.semaphore_signal(barrier, inc=1, device_id={"row": (band + step) % rows})

    for p in range(heads // 2):
        lanes = slice(p * PAIR, (p + 1) * PAIR)
        keys, values = k_ref[:, lanes], v_ref[:, lanes]
        left = jnp.concatenate([keys[:, :HEAD_DIM], values[:, :HEAD_DIM]], axis=1)
        right = jnp.concatenate([keys[:, HEAD_DIM:], values[:, HEAD_DIM:]], axis=1)
        kv_pack[2 * p] = left.reshape(blocks, BLOCK, PAIR)
        kv_pack[2 * p + 1] = right.reshape(blocks, BLOCK, PAIR)
    flags = [(me // 2 ** (levels - 1 - d)) % 2 for d in range(levels)]
    here = tuple(pl.ds(flag, 1) for flag in flags)
    for j in range(blocks):
        words = bits_ref[j * BLOCK : (j + 1) * BLOCK, :].astype(jnp.float32).T.astype(jnp.bfloat16)
        bits_all[here + (j,)] = words.reshape((1,) * levels + words.shape)

    pl.semaphore_wait(barrier, cols - 1 + rows - 1)

    def kv_copy(turn):
        step = (turn * stride_of(cols)) % cols
        other = (me + step) % cols
        return pltpu.make_async_remote_copy(
            src_ref=kv_pack.at[other % heads],
            dst_ref=kv_in.at[turn],
            send_sem=kv_send.at[step],
            recv_sem=kv_recv.at[step],
            device_id={"col": other},
        )

    def kv_start(turn, carry):
        kv_copy(turn).start()
        return carry

    bounds = [1 + (cols - 1) * i // levels for i in range(levels + 1)]

    def bits_copy(dim):
        bit = levels - 1 - dim
        region = (slice(None),) * dim + here[dim:]
        return pltpu.make_async_remote_copy(
            src_ref=bits_all.at[region],
            dst_ref=bits_all.at[region],
            send_sem=bit_send.at[dim],
            recv_sem=bit_recv.at[dim],
            device_id={"col": me + 2**bit - 2 * 2**bit * flags[dim]},
        )

    for dim in range(levels):
        copy = bits_copy(dim)
        copy.start()
        lax.fori_loop(bounds[dim], bounds[dim + 1], kv_start, 0)
        if dim == 0:
            for p in range(heads // 2):
                lanes = slice(p * PAIR, (p + 1) * PAIR)
                query = (q_ref[:, lanes].astype(jnp.float32) * score_scale).astype(jnp.bfloat16)
                grad = g_ref[:, lanes]
                qg_pack[2 * p] = jnp.concatenate([query[:, :HEAD_DIM], grad[:, :HEAD_DIM]], axis=1)
                qg_pack[2 * p + 1] = jnp.concatenate([query[:, HEAD_DIM:], grad[:, HEAD_DIM:]], axis=1)
        copy.wait()

    def qg_copy(turn):
        step = (turn * stride_of(heads)) % heads
        other = (head + step) % heads
        return pltpu.make_async_remote_copy(
            src_ref=qg_pack.at[other],
            dst_ref=qg_in.at[turn],
            send_sem=qg_send.at[step],
            recv_sem=qg_recv.at[step],
            device_id={"col": group * heads + other},
        )

    def qg_start(turn, carry):
        qg_copy(turn).start()
        return carry

    lax.fori_loop(1, heads, qg_start, 0)
    qg_in[0] = qg_pack[head]

    def find(place, carry):
        for r in range(NMATCH):
            def look(c, found):
                return found + jnp.where(partner_ref[r, band, c] == place, c, 0)

            inverse_ref[r, place] = jnp.minimum(lax.fori_loop(0, cols, look, 0), cols - 1)
        return carry

    lax.fori_loop(0, cols, find, 0)

    def clear(i, carry):
        acc_ref[i] = jnp.zeros((BLOCK, PAIR), jnp.float32)
        return carry

    lax.fori_loop(0, last + 2, clear, 0)
    gacc_ref[...] = jnp.zeros_like(gacc_ref)

    def turn_block(value):
        return value.astype(jnp.float32).T.astype(jnp.bfloat16)

    def place_kv(turn):
        source = (me + turn * (cols - stride_of(cols))) % cols
        for j in range(blocks):
            value = kv_in[turn, j]
            kv_ext[1 + source * blocks + j] = value
            kv_turned[1 + source * blocks + j] = turn_block(value)

    kv_in[0] = kv_pack[head]
    place_kv(0)

    def kv_take(turn, carry):
        kv_copy(turn).wait()
        place_kv(turn)
        return carry

    lax.fori_loop(1, cols, kv_take, 0)

    def edge_copies():
        return [
            pltpu.make_async_remote_copy(
                src_ref=kv_ext.at[last],
                dst_ref=halo.at[0],
                send_sem=row_send.at[0],
                recv_sem=row_recv.at[0],
                device_id={"row": (band + 1) % rows},
            ),
            pltpu.make_async_remote_copy(
                src_ref=kv_ext.at[1],
                dst_ref=halo.at[1],
                send_sem=row_send.at[1],
                recv_sem=row_recv.at[1],
                device_id={"row": (band + rows - 1) % rows},
            ),
        ]

    def shared_copy(step):
        return pltpu.make_async_remote_copy(
            src_ref=shared.at[band],
            dst_ref=shared.at[band],
            send_sem=row_send.at[1 + step],
            recv_sem=row_recv.at[1 + step],
            device_id={"row": (band + step) % rows},
        )

    for n in range(NGLOBAL):
        shared[band, n] = kv_ext[1 + jnp.clip(global_ref[n] - band * last, 0, last - 1)]
    for copy in edge_copies():
        copy.start()
    for step in range(1, rows):
        shared_copy(step).start()
    for copy in edge_copies():
        copy.wait()
    for side, place in ((0, 0), (1, last + 1)):
        value = halo[side]
        kv_ext[place] = value
        kv_turned[place] = turn_block(value)
    for step in range(1, rows):
        shared_copy(step).wait()
    for n in range(NGLOBAL):
        value = shared[global_ref[n] // last, n]
        shared_keys[n] = value
        shared_turned[n] = turn_block(value)

    for slot in range(heads):
        where_bits = tuple((slot // 2 ** (levels - 1 - d)) % 2 for d in range(levels))
        words_ref[slot] = bits_all[where_bits].astype(jnp.float32).astype(jnp.int32)

    wide = 2 * BLOCK
    marks = jnp.left_shift(1, lax.broadcasted_iota(jnp.int32, (BLOCK // 8, 8, BLOCK), 1))

    def attend(turn):
        slot = (head + turn * (heads - stride_of(heads))) % heads
        place = group * heads + slot
        far = [1 + partner_ref[r, band, place] * blocks + pick_ref[r, band, place] for r in range(NMATCH)]
        far_keys = [shared_keys[n] for n in range(NGLOBAL)] + [kv_ext[b] for b in far]
        near_keys = [kv_ext[place * blocks + b] for b in range(blocks + 2)]
        sides = []
        for j in range(blocks):
            packed = qg_in[turn, j * BLOCK : (j + 1) * BLOCK, :]
            side = jnp.concatenate([jnp.where(first, packed, zero), jnp.where(first, zero, packed)], axis=0)
            sides.append(side)
            keys = near_keys[j : j + 3] + far_keys
            top = None
            for i in range(SLOTS):
                both = contract(keys[i], side, 1, 1)
                s_ref[i] = both
                part = jnp.max(both[:, :BLOCK].reshape(BLOCK // 8, 8, BLOCK), axis=0)
                top = part if top is None else jnp.maximum(top, part)
            top = jnp.max(top, axis=0, keepdims=True)
            total, mixed = None, None
            for i in range(SLOTS):
                words = words_ref[slot, j, i * BLOCK // 8 : (i + 1) * BLOCK // 8, :]
                keep = (jnp.broadcast_to(words[:, None, :], marks.shape) & marks) != 0
                weight = jnp.exp(s_ref[i, :, :BLOCK] - top).reshape(marks.shape)
                grad_p = jnp.where(keep, s_ref[i, :, BLOCK:].reshape(marks.shape), 0.0)
                s_ref[i, :, :BLOCK] = weight.reshape(BLOCK, BLOCK)
                s_ref[i, :, BLOCK:] = grad_p.reshape(BLOCK, BLOCK)
                part = jnp.sum(weight, axis=0)
                cross = jnp.sum(weight * grad_p, axis=0)
                total = part if total is None else total + part
                mixed = cross if mixed is None else mixed + cross
            inverse = 1.0 / jnp.sum(total, axis=0, keepdims=True)
            delta = jnp.sum(mixed, axis=0, keepdims=True) * inverse
            scaled = inverse * keep_scale
            for i in range(SLOTS):
                words = words_ref[slot, j, i * BLOCK // 8 : (i + 1) * BLOCK // 8, :]
                keep = (jnp.broadcast_to(words[:, None, :], marks.shape) & marks) != 0
                probs = s_ref[i, :, :BLOCK] * scaled
                dscore = probs * (s_ref[i, :, BLOCK:] - delta)
                dropped = jnp.where(keep, probs.reshape(marks.shape), 0.0).reshape(BLOCK, BLOCK)
                dsp_ref[j, i, :, :BLOCK] = dscore.astype(jnp.bfloat16)
                dsp_ref[j, i, :, BLOCK:] = dropped.astype(jnp.bfloat16)
            turned = [kv_turned[place * blocks + j + b] for b in range(3)]
            turned += [shared_turned[n] for n in range(NGLOBAL)] + [kv_turned[b] for b in far]
            out = contract(jnp.concatenate(turned, axis=1), dsp_ref[j].reshape(SLOTS * BLOCK, wide), 1, 0)
            out = jnp.concatenate([out[:HEAD_DIM, :BLOCK] * score_scale, out[HEAD_DIM:, BLOCK:]], axis=0)
            qa_out[turn, j * BLOCK : (j + 1) * BLOCK, :] = out.T.astype(jnp.bfloat16)
        for j in range(blocks):
            grads = contract(dsp_ref[j, :3].reshape(3 * BLOCK, wide), sides[j], 1, 0)
            for b in range(3):
                acc_ref[place * blocks + j + b] += grads[b * BLOCK : (b + 1) * BLOCK]
        grads = None
        for j in range(blocks):
            part = contract(dsp_ref[j, 3:].reshape((SLOTS - 3) * BLOCK, wide), sides[j], 1, 0)
            grads = part if grads is None else grads + part
        for n in range(NGLOBAL):
            gacc_ref[n] += grads[n * BLOCK : (n + 1) * BLOCK]
        for r in range(NMATCH):
            rand_ref[slot, r] = grads[(NGLOBAL + r) * BLOCK : (NGLOBAL + r + 1) * BLOCK]

    def qa_copy(turn):
        step = (turn * stride_of(heads)) % heads
        slot = (head - step + heads) % heads
        return pltpu.make_async_remote_copy(
            src_ref=qa_out.at[turn],
            dst_ref=qa_land.at[head],
            send_sem=qa_send.at[step],
            recv_sem=qa_recv.at[step],
            device_id={"col": group * heads + slot},
        )

    def segment(turn, carry):
        qg_copy(turn).wait()
        attend(turn)
        qa_copy(turn).start()
        return carry

    attend(0)
    lax.fori_loop(1, heads, segment, 0)
    qa_land[head] = qa_out[0]

    def back_copies():
        copies = [
            pltpu.make_async_remote_copy(
                src_ref=acc_ref.at[last + 1],
                dst_ref=halo_acc.at[0],
                send_sem=back_send.at[0],
                recv_sem=back_recv.at[0],
                device_id={"row": (band + 1) % rows},
            ),
            pltpu.make_async_remote_copy(
                src_ref=acc_ref.at[0],
                dst_ref=halo_acc.at[1],
                send_sem=back_send.at[1],
                recv_sem=back_recv.at[1],
                device_id={"row": (band + rows - 1) % rows},
            ),
        ]
        for step in range(1, rows):
            copies.append(
                pltpu.make_async_remote_copy(
                    src_ref=gacc_ref,
                    dst_ref=gacc_in.at[band],
                    send_sem=back_send.at[1 + step],
                    recv_sem=back_recv.at[1 + step],
                    device_id={"row": (band + step) % rows},
                )
            )
        return copies

    for copy in back_copies():
        copy.start()
    for copy in back_copies():
        copy.wait()
    sums = []
    for n in range(NGLOBAL):
        total = gacc_ref[n]
        for step in range(1, rows):
            total = total + gacc_in[(band + step) % rows, n]
        s_ref[n, :, :BLOCK] = total
    acc_ref[1] += halo_acc[0]
    acc_ref[last] += halo_acc[1]

    def collect(turn):
        place = (me + turn * stride_of(cols)) % cols
        totals = [acc_ref[1 + place * blocks + j] for j in range(blocks)]
        for r in range(NMATCH):
            source = inverse_ref[r, place]
            chosen = jnp.where(source // heads == group, pick_ref[r, band, source], blocks)
            part = rand_ref[source % heads, r]
            totals = [total + jnp.where(chosen == j, part, 0.0) for j, total in enumerate(totals)]
        for n in range(NGLOBAL):
            chosen = global_ref[n] - (band * cols + place) * blocks
            part = s_ref[n, :, :BLOCK]
            totals = [total + jnp.where(chosen == j, part, 0.0) for j, total in enumerate(totals)]
        for j in range(blocks):
            kvg_out[turn, j] = totals[j].astype(jnp.bfloat16)

    def kvg_copy(turn):
        step = (turn * stride_of(cols)) % cols
        other = (me + step) % cols
        return pltpu.make_async_remote_copy(
            src_ref=kvg_out.at[turn],
            dst_ref=kvg_land.at[me],
            send_sem=kvg_send.at[step],
            recv_sem=kvg_recv.at[step],
            device_id={"col": other},
        )

    def give(turn, carry):
        collect(turn)
        kvg_copy(turn).start()
        return carry

    lax.fori_loop(1, cols, give, 0)
    collect(0)
    kvg_land[me] = kvg_out[0]

    def qa_finish(turn, carry):
        qa_copy(turn).wait()
        return carry

    lax.fori_loop(1, heads, qa_finish, 0)

    def kvg_finish(turn, carry):
        kvg_copy(turn).wait()
        return carry

    lax.fori_loop(1, cols, kvg_finish, 0)


def fused(rows, cols, queries, key_rows, value_rows, out_grad, bits, partner, pick, shared_ids):
    tokens_here, width = queries.shape
    blocks = tokens_here // BLOCK
    heads = width // HEAD_DIM
    levels = heads.bit_length() - 1
    last = cols * blocks
    half, full = jnp.bfloat16, jnp.float32
    vmem = pl.BlockSpec(memory_space=pltpu.VMEM)
    smem = pl.BlockSpec(memory_space=pltpu.SMEM)

    scratch = [
        pltpu.VMEM((heads, blocks, BLOCK, PAIR), half),
        pltpu.VMEM((heads, tokens_here, PAIR), half),
        pltpu.VMEM((cols, blocks, BLOCK, PAIR), half),
        pltpu.VMEM((heads, tokens_here, PAIR), half),
        pltpu.VMEM((2,) * levels + (blocks, BLOCK, BLOCK), half),
        pltpu.VMEM((last + 2, BLOCK, PAIR), half),
        pltpu.VMEM((last + 2, PAIR, BLOCK), half),
        pltpu.VMEM((2, BLOCK, PAIR), half),
        pltpu.VMEM((rows, NGLOBAL, BLOCK, PAIR), half),
        pltpu.VMEM((NGLOBAL, PAIR, BLOCK), half),
        pltpu.VMEM((NGLOBAL, BLOCK, PAIR), half),
        pltpu.VMEM((heads, blocks, BLOCK, BLOCK), jnp.int32),
        pltpu.VMEM((SLOTS, BLOCK, 2 * BLOCK), full),
        pltpu.VMEM((blocks, SLOTS, BLOCK, 2 * BLOCK), half),
        pltpu.VMEM((last + 2, BLOCK, PAIR), full),
        pltpu.VMEM((heads, NMATCH, BLOCK, PAIR), full),
        pltpu.VMEM((NGLOBAL, BLOCK, PAIR), full),
        pltpu.VMEM((2, BLOCK, PAIR), full),
        pltpu.VMEM((rows, NGLOBAL, BLOCK, PAIR), full),
        pltpu.VMEM((heads, tokens_here, PAIR), half),
        pltpu.VMEM((cols, blocks, BLOCK, PAIR), half),
        pltpu.SMEM((NMATCH, cols), jnp.int32),
    ]
    for count in (cols, heads, levels, rows + 1, rows + 1, heads, cols):
        scratch += [pltpu.SemaphoreType.DMA((count,))] * 2
    return pl.pallas_call(
        functools.partial(fused_kernel, rows, cols, heads, blocks),
        out_shape=[
            jax.ShapeDtypeStruct((heads, tokens_here, PAIR), half),
            jax.ShapeDtypeStruct((cols, blocks, BLOCK, PAIR), half),
        ],
        in_specs=[vmem] * 5 + [smem] * 3,
        out_specs=[vmem, vmem],
        scratch_shapes=scratch,
        compiler_params=pltpu.CompilerParams(collective_id=1, has_side_effects=True),
        name="head_attention",
    )(queries, key_rows, value_rows, out_grad, bits, partner, pick, shared_ids)


def unpack_kernel(groups, qa_ref, kvg_ref, att_ref, qg_ref, kg_ref, vg_ref):
    def split(pairs):
        left, right = pairs
        low = jnp.concatenate([left[:, :HEAD_DIM], right[:, :HEAD_DIM]], axis=1)
        high = jnp.concatenate([left[:, HEAD_DIM:], right[:, HEAD_DIM:]], axis=1)
        return low, high

    qg_ref[...], att_ref[...] = split([qa_ref[0], qa_ref[1]])
    totals = []
    for side in range(2):
        total = kvg_ref[0, side]
        if groups > 1:
            total = total.astype(jnp.float32)
            for g in range(1, groups):
                total = total + kvg_ref[g, side].astype(jnp.float32)
            total = total.astype(jnp.bfloat16)
        totals.append(total)
    kg_ref[...], vg_ref[...] = split(totals)


def unpack(qa, kvg):
    heads, tokens_here, _ = qa.shape
    groups = kvg.shape[0] // heads
    kvg = kvg.reshape(groups, heads, tokens_here, PAIR)
    flat = pl.BlockSpec((tokens_here, PAIR), lambda p: (0, p))
    shape = jax.ShapeDtypeStruct((tokens_here, heads * HEAD_DIM), jnp.bfloat16)
    return pl.pallas_call(
        functools.partial(unpack_kernel, groups),
        grid=(heads // 2,),
        in_specs=[
            pl.BlockSpec((2, tokens_here, PAIR), lambda p: (p, 0, 0)),
            pl.BlockSpec((groups, 2, tokens_here, PAIR), lambda p: (0, p, 0, 0)),
        ],
        out_specs=[flat] * 4,
        out_shape=[shape] * 4,
        name="unpack_heads",
    )(qa, kvg)


def body(queries, key_rows, value_rows, out_grad, dropout_bits, partner, block_pick, global_blocks):
    rows, cols = lax.axis_size("row"), lax.axis_size("col")
    qa, kvg = fused(
        rows, cols, queries, key_rows, value_rows, out_grad, dropout_bits, partner, block_pick, global_blocks
    )
    attended, query_grad, key_grad, value_grad = unpack(qa, kvg)
    return attended, query_grad, key_grad, value_grad


def solution(mesh):
    split = P(("row", "col"), None)
    return jax.shard_map(
        body,
        mesh=mesh,
        in_specs=(split,) * 5 + (P(),) * 3,
        out_specs=(split,) * 4,
        check_vma=False,
    )
```

```python
import functools

import jax
import jax.numpy as jnp
from jax import lax
from jax.experimental import pallas as pl
from jax.experimental.pallas import tpu as pltpu
from jax.sharding import PartitionSpec as P

HEAD_DIM = 64
BLOCK = 128
NGLOBAL = 2
NMATCH = 3
PAIR = 2 * HEAD_DIM

score_scale = 0.125
keep_scale = 1.0 / 0.9


def contract(a, b, dim_a, dim_b):
    return lax.dot_general(a, b, (((dim_a,), (dim_b,)), ((), ())), preferred_element_type=jnp.float32)


def stride_of(count):
    return max(1, count // 2 - 1)


def fused_kernel(
    rows, cols, heads, blocks,
    q_ref, k_ref, v_ref, g_ref, bits_ref, partner_ref, pick_ref, global_ref,
    qa_land, kvg_land,
    kv_pack, qg_pack, kv_in, qg_in, bits_all, kv_ext, kv_turned, halo, shared, shared_turned,
    shared_keys, words_ref, s_ref, u_ref, p_ref, ds_ref, acc_ref, rand_ref, gacc_ref, halo_acc, gacc_in, qa_out, kvg_out, inverse_ref,
    kv_send, kv_recv, qg_send, qg_recv, bit_send, bit_recv, row_send, row_recv, back_send, back_recv, qa_send, qa_recv, kvg_send, kvg_recv,
):
    me, band = lax.axis_index("col"), lax.axis_index("row")
    head, group = me % heads, me // heads
    levels = heads.bit_length() - 1
    last = cols * blocks
    first = lax.broadcasted_iota(jnp.int32, (BLOCK, PAIR), 1) < HEAD_DIM
    zero = jnp.zeros((BLOCK, PAIR), jnp.bfloat16)

    barrier = pltpu.get_barrier_semaphore()

    def hello(step, carry):
        pl.semaphore_signal(barrier, inc=1, device_id={"col": (me + step) % cols})
        return carry

    lax.fori_loop(1, cols, hello, 0)
    for step in range(1, rows):
        pl.semaphore_signal(barrier, inc=1, device_id={"row": (band + step) % rows})

    for p in range(heads // 2):
        lanes = slice(p * PAIR, (p + 1) * PAIR)
        keys, values = k_ref[:, lanes], v_ref[:, lanes]
        left = jnp.concatenate([keys[:, :HEAD_DIM], values[:, :HEAD_DIM]], axis=1)
        right = jnp.concatenate([keys[:, HEAD_DIM:], values[:, HEAD_DIM:]], axis=1)
        kv_pack[2 * p] = left.reshape(blocks, BLOCK, PAIR)
        kv_pack[2 * p + 1] = right.reshape(blocks, BLOCK, PAIR)
    flags = [(me // 2 ** (levels - 1 - d)) % 2 for d in range(levels)]
    here = tuple(pl.ds(flag, 1) for flag in flags)
    for j in range(blocks):
        words = bits_ref[j * BLOCK : (j + 1) * BLOCK, :].astype(jnp.float32).T.astype(jnp.bfloat16)
        bits_all[here + (j,)] = words.reshape((1,) * levels + words.shape)

    pl.semaphore_wait(barrier, cols - 1 + rows - 1)

    def kv_copy(turn):
        step = (turn * stride_of(cols)) % cols
        other = (me + step) % cols
        return pltpu.make_async_remote_copy(
            src_ref=kv_pack.at[other % heads],
            dst_ref=kv_in.at[turn],
            send_sem=kv_send.at[step],
            recv_sem=kv_recv.at[step],
            device_id={"col": other},
        )

    def kv_start(turn, carry):
        kv_copy(turn).start()
        return carry

    bounds = [1 + (cols - 1) * i // levels for i in range(levels + 1)]

    def bits_copy(dim):
        bit = levels - 1 - dim
        region = (slice(None),) * dim + here[dim:]
        return pltpu.make_async_remote_copy(
            src_ref=bits_all.at[region],
            dst_ref=bits_all.at[region],
            send_sem=bit_send.at[dim],
            recv_sem=bit_recv.at[dim],
            device_id={"col": me + 2**bit - 2 * 2**bit * flags[dim]},
        )

    for dim in range(levels):
        copy = bits_copy(dim)
        copy.start()
        lax.fori_loop(bounds[dim], bounds[dim + 1], kv_start, 0)
        if dim == 0:
            for p in range(heads // 2):
                lanes = slice(p * PAIR, (p + 1) * PAIR)
                query = (q_ref[:, lanes].astype(jnp.float32) * score_scale).astype(jnp.bfloat16)
                grad = g_ref[:, lanes]
                qg_pack[2 * p] = jnp.concatenate([query[:, :HEAD_DIM], grad[:, :HEAD_DIM]], axis=1)
                qg_pack[2 * p + 1] = jnp.concatenate([query[:, HEAD_DIM:], grad[:, HEAD_DIM:]], axis=1)
        copy.wait()

    def qg_copy(turn):
        step = (turn * stride_of(heads)) % heads
        other = (head + step) % heads
        return pltpu.make_async_remote_copy(
            src_ref=qg_pack.at[other],
            dst_ref=qg_in.at[turn],
            send_sem=qg_send.at[step],
            recv_sem=qg_recv.at[step],
            device_id={"col": group * heads + other},
        )

    def qg_start(turn, carry):
        qg_copy(turn).start()
        return carry

    lax.fori_loop(1, heads, qg_start, 0)
    qg_in[0] = qg_pack[head]

    def find(place, carry):
        for r in range(NMATCH):
            def look(c, found):
                return found + jnp.where(partner_ref[r, band, c] == place, c, 0)

            inverse_ref[r, place] = jnp.minimum(lax.fori_loop(0, cols, look, 0), cols - 1)
        return carry

    lax.fori_loop(0, cols, find, 0)

    def clear(i, carry):
        acc_ref[i] = jnp.zeros((BLOCK, PAIR), jnp.float32)
        return carry

    lax.fori_loop(0, last + 2, clear, 0)
    gacc_ref[...] = jnp.zeros_like(gacc_ref)

    def turn_block(value):
        return value.astype(jnp.float32).T.astype(jnp.bfloat16)

    def place_kv(turn):
        source = (me + turn * (cols - stride_of(cols))) % cols
        for j in range(blocks):
            value = kv_in[turn, j]
            kv_ext[1 + source * blocks + j] = value
            kv_turned[1 + source * blocks + j] = turn_block(value)

    kv_in[0] = kv_pack[head]
    place_kv(0)

    def kv_take(turn, carry):
        kv_copy(turn).wait()
        place_kv(turn)
        return carry

    lax.fori_loop(1, cols, kv_take, 0)

    def edge_copies():
        return [
            pltpu.make_async_remote_copy(
                src_ref=kv_ext.at[last],
                dst_ref=halo.at[0],
                send_sem=row_send.at[0],
                recv_sem=row_recv.at[0],
                device_id={"row": (band + 1) % rows},
            ),
            pltpu.make_async_remote_copy(
                src_ref=kv_ext.at[1],
                dst_ref=halo.at[1],
                send_sem=row_send.at[1],
                recv_sem=row_recv.at[1],
                device_id={"row": (band + rows - 1) % rows},
            ),
        ]

    def shared_copy(step):
        return pltpu.make_async_remote_copy(
            src_ref=shared.at[band],
            dst_ref=shared.at[band],
            send_sem=row_send.at[1 + step],
            recv_sem=row_recv.at[1 + step],
            device_id={"row": (band + step) % rows},
        )

    for n in range(NGLOBAL):
        shared[band, n] = kv_ext[1 + jnp.clip(global_ref[n] - band * last, 0, last - 1)]
    for copy in edge_copies():
        copy.start()
    for step in range(1, rows):
        shared_copy(step).start()
    for copy in edge_copies():
        copy.wait()
    for side, place in ((0, 0), (1, last + 1)):
        value = halo[side]
        kv_ext[place] = value
        kv_turned[place] = turn_block(value)
    for step in range(1, rows):
        shared_copy(step).wait()
    for n in range(NGLOBAL):
        value = shared[global_ref[n] // last, n]
        shared_keys[n] = value
        shared_turned[n] = turn_block(value)

    for slot in range(heads):
        where_bits = tuple((slot // 2 ** (levels - 1 - d)) % 2 for d in range(levels))
        words_ref[slot] = bits_all[where_bits].astype(jnp.float32).astype(jnp.int32)

    wide = blocks * BLOCK
    reach = blocks + 2
    marks = jnp.left_shift(1, lax.broadcasted_iota(jnp.int32, (BLOCK // 8, 8, BLOCK), 1))
    p_ref[...] = jnp.zeros_like(p_ref)
    ds_ref[...] = jnp.zeros_like(ds_ref)
    first_all = lax.broadcasted_iota(jnp.int32, (wide, PAIR), 1) < HEAD_DIM
    zero_all = jnp.zeros((wide, PAIR), jnp.bfloat16)

    def attend(turn):
        slot = (head + turn * (heads - stride_of(heads))) % heads
        place = group * heads + slot
        far = [1 + partner_ref[r, band, place] * blocks + pick_ref[r, band, place] for r in range(NMATCH)]
        keys = [kv_ext[place * blocks + b] for b in range(reach)]
        keys += [shared_keys[n] for n in range(NGLOBAL)] + [kv_ext[b] for b in far]
        seen = [[(j, b - j) for j in range(blocks) if 0 <= b - j < 3] for b in range(reach)]
        seen += [[(j, 3 + f) for j in range(blocks)] for f in range(NGLOBAL + NMATCH)]
        packed = qg_in[turn]
        side_q = jnp.where(first_all, packed, zero_all)
        side_g = jnp.where(first_all, zero_all, packed)
        tops = [None] * blocks
        for b, pairs in enumerate(seen):
            lower, upper = pairs[0][0] * BLOCK, (pairs[-1][0] + 1) * BLOCK
            score = contract(keys[b], side_q[lower:upper], 1, 1)
            s_ref[b, :, lower:upper] = score
            for j, _ in pairs:
                tile = score[:, j * BLOCK - lower : (j + 1) * BLOCK - lower]
                part = jnp.max(tile.reshape(BLOCK // 8, 8, BLOCK), axis=0)
                tops[j] = part if tops[j] is None else jnp.maximum(tops[j], part)
        tops = [jnp.max(top, axis=0, keepdims=True) for top in tops]
        totals, mixed = [0.0] * blocks, [0.0] * blocks
        for b, pairs in enumerate(seen):
            lower, upper = pairs[0][0] * BLOCK, (pairs[-1][0] + 1) * BLOCK
            grad_p = contract(keys[b], side_g[lower:upper], 1, 1)
            for j, i in pairs:
                cols_j = slice(j * BLOCK, (j + 1) * BLOCK)
                words = words_ref[slot, j, i * BLOCK // 8 : (i + 1) * BLOCK // 8, :]
                keep = (jnp.broadcast_to(words[:, None, :], marks.shape) & marks) != 0
                weight = jnp.exp(s_ref[b, :, cols_j] - tops[j]).reshape(marks.shape)
                kept = jnp.where(keep, weight, 0.0)
                cross = kept * grad_p[:, j * BLOCK - lower : (j + 1) * BLOCK - lower].reshape(marks.shape)
                s_ref[b, :, cols_j] = weight.reshape(BLOCK, BLOCK)
                u_ref[b, :, cols_j] = cross.reshape(BLOCK, BLOCK)
                p_ref[b, :, cols_j] = kept.reshape(BLOCK, BLOCK).astype(jnp.bfloat16)
                totals[j] = totals[j] + jnp.sum(weight, axis=0)
                mixed[j] = mixed[j] + jnp.sum(cross, axis=0)
        scales, deltas = [], []
        for j in range(blocks):
            inverse = 1.0 / jnp.sum(totals[j], axis=0, keepdims=True)
            deltas.append(jnp.sum(mixed[j], axis=0, keepdims=True) * inverse)
            scales.append(inverse * keep_scale)
        for b, pairs in enumerate(seen):
            for j, _ in pairs:
                cols_j = slice(j * BLOCK, (j + 1) * BLOCK)
                ds_ref[b, :, cols_j] = (u_ref[b, :, cols_j] - s_ref[b, :, cols_j] * deltas[j]).astype(jnp.bfloat16)
        turned = [kv_turned[place * blocks + b] for b in range(reach)]
        turned += [shared_turned[n] for n in range(NGLOBAL)] + [kv_turned[b] for b in far]
        turned = jnp.concatenate(turned, axis=1)
        whole = (reach + NGLOBAL + NMATCH) * BLOCK
        out_p = contract(turned, p_ref[...].reshape(whole, wide), 1, 0)
        out_s = contract(turned, ds_ref[...].reshape(whole, wide), 1, 0)
        factors = []
        for j in range(blocks):
            cols_j = slice(j * BLOCK, (j + 1) * BLOCK)
            out = jnp.concatenate(
                [out_s[:HEAD_DIM, cols_j] * (scales[j] * score_scale), out_p[HEAD_DIM:, cols_j] * scales[j]], axis=0
            )
            qa_out[turn, cols_j, :] = out.T.astype(jnp.bfloat16)
            factors.append(jnp.broadcast_to(scales[j], (BLOCK, BLOCK)).T)
        scaled = (packed.astype(jnp.float32) * jnp.concatenate(factors, axis=0)).astype(jnp.bfloat16)
        grads = contract(ds_ref[...].reshape(whole, wide), jnp.where(first_all, scaled, zero_all), 1, 0)
        grads = grads + contract(p_ref[...].reshape(whole, wide), jnp.where(first_all, zero_all, scaled), 1, 0)
        for b in range(reach):
            acc_ref[place * blocks + b] += grads[b * BLOCK : (b + 1) * BLOCK]
        base = reach * BLOCK
        for n in range(NGLOBAL):
            gacc_ref[n] += grads[base + n * BLOCK : base + (n + 1) * BLOCK]
        base += NGLOBAL * BLOCK
        for r in range(NMATCH):
            rand_ref[slot, r] = grads[base + r * BLOCK : base + (r + 1) * BLOCK]

    def qa_copy(turn):
        step = (turn * stride_of(heads)) % heads
        slot = (head - step + heads) % heads
        return pltpu.make_async_remote_copy(
            src_ref=qa_out.at[turn],
            dst_ref=qa_land.at[head],
            send_sem=qa_send.at[step],
            recv_sem=qa_recv.at[step],
            device_id={"col": group * heads + slot},
        )

    def segment(turn, carry):
        qg_copy(turn).wait()
        attend(turn)
        qa_copy(turn).start()
        return carry

    attend(0)
    lax.fori_loop(1, heads, segment, 0)
    qa_land[head] = qa_out[0]

    def back_copies():
        copies = [
            pltpu.make_async_remote_copy(
                src_ref=acc_ref.at[last + 1],
                dst_ref=halo_acc.at[0],
                send_sem=back_send.at[0],
                recv_sem=back_recv.at[0],
                device_id={"row": (band + 1) % rows},
            ),
            pltpu.make_async_remote_copy(
                src_ref=acc_ref.at[0],
                dst_ref=halo_acc.at[1],
                send_sem=back_send.at[1],
                recv_sem=back_recv.at[1],
                device_id={"row": (band + rows - 1) % rows},
            ),
        ]
        for step in range(1, rows):
            copies.append(
                pltpu.make_async_remote_copy(
                    src_ref=gacc_ref,
                    dst_ref=gacc_in.at[band],
                    send_sem=back_send.at[1 + step],
                    recv_sem=back_recv.at[1 + step],
                    device_id={"row": (band + step) % rows},
                )
            )
        return copies

    for copy in back_copies():
        copy.start()
    for copy in back_copies():
        copy.wait()
    sums = []
    for n in range(NGLOBAL):
        total = gacc_ref[n]
        for step in range(1, rows):
            total = total + gacc_in[(band + step) % rows, n]
        s_ref[n, :, :BLOCK] = total
    acc_ref[1] += halo_acc[0]
    acc_ref[last] += halo_acc[1]

    def collect(turn):
        place = (me + turn * stride_of(cols)) % cols
        totals = [acc_ref[1 + place * blocks + j] for j in range(blocks)]
        for r in range(NMATCH):
            source = inverse_ref[r, place]
            chosen = jnp.where(source // heads == group, pick_ref[r, band, source], blocks)
            part = rand_ref[source % heads, r]
            totals = [total + jnp.where(chosen == j, part, 0.0) for j, total in enumerate(totals)]
        for n in range(NGLOBAL):
            chosen = global_ref[n] - (band * cols + place) * blocks
            part = s_ref[n, :, :BLOCK]
            totals = [total + jnp.where(chosen == j, part, 0.0) for j, total in enumerate(totals)]
        for j in range(blocks):
            kvg_out[turn, j] = totals[j].astype(jnp.bfloat16)

    def kvg_copy(turn):
        step = (turn * stride_of(cols)) % cols
        other = (me + step) % cols
        return pltpu.make_async_remote_copy(
            src_ref=kvg_out.at[turn],
            dst_ref=kvg_land.at[me],
            send_sem=kvg_send.at[step],
            recv_sem=kvg_recv.at[step],
            device_id={"col": other},
        )

    def give(turn, carry):
        collect(turn)
        kvg_copy(turn).start()
        return carry

    lax.fori_loop(1, cols, give, 0)
    collect(0)
    kvg_land[me] = kvg_out[0]

    def qa_finish(turn, carry):
        qa_copy(turn).wait()
        return carry

    lax.fori_loop(1, heads, qa_finish, 0)

    def kvg_finish(turn, carry):
        kvg_copy(turn).wait()
        return carry

    lax.fori_loop(1, cols, kvg_finish, 0)


def fused(rows, cols, queries, key_rows, value_rows, out_grad, bits, partner, pick, shared_ids):
    tokens_here, width = queries.shape
    blocks = tokens_here // BLOCK
    heads = width // HEAD_DIM
    levels = heads.bit_length() - 1
    last = cols * blocks
    tiles = blocks + 2 + NGLOBAL + NMATCH
    half, full = jnp.bfloat16, jnp.float32
    vmem = pl.BlockSpec(memory_space=pltpu.VMEM)
    smem = pl.BlockSpec(memory_space=pltpu.SMEM)

    scratch = [
        pltpu.VMEM((heads, blocks, BLOCK, PAIR), half),
        pltpu.VMEM((heads, tokens_here, PAIR), half),
        pltpu.VMEM((cols, blocks, BLOCK, PAIR), half),
        pltpu.VMEM((heads, tokens_here, PAIR), half),
        pltpu.VMEM((2,) * levels + (blocks, BLOCK, BLOCK), half),
        pltpu.VMEM((last + 2, BLOCK, PAIR), half),
        pltpu.VMEM((last + 2, PAIR, BLOCK), half),
        pltpu.VMEM((2, BLOCK, PAIR), half),
        pltpu.VMEM((rows, NGLOBAL, BLOCK, PAIR), half),
        pltpu.VMEM((NGLOBAL, PAIR, BLOCK), half),
        pltpu.VMEM((NGLOBAL, BLOCK, PAIR), half),
        pltpu.VMEM((heads, blocks, BLOCK, BLOCK), jnp.int32),
        pltpu.VMEM((tiles, BLOCK, tokens_here), full),
        pltpu.VMEM((tiles, BLOCK, tokens_here), full),
        pltpu.VMEM((tiles, BLOCK, tokens_here), half),
        pltpu.VMEM((tiles, BLOCK, tokens_here), half),
        pltpu.VMEM((last + 2, BLOCK, PAIR), full),
        pltpu.VMEM((heads, NMATCH, BLOCK, PAIR), full),
        pltpu.VMEM((NGLOBAL, BLOCK, PAIR), full),
        pltpu.VMEM((2, BLOCK, PAIR), full),
        pltpu.VMEM((rows, NGLOBAL, BLOCK, PAIR), full),
        pltpu.VMEM((heads, tokens_here, PAIR), half),
        pltpu.VMEM((cols, blocks, BLOCK, PAIR), half),
        pltpu.SMEM((NMATCH, cols), jnp.int32),
    ]
    for count in (cols, heads, levels, rows + 1, rows + 1, heads, cols):
        scratch += [pltpu.SemaphoreType.DMA((count,))] * 2
    return pl.pallas_call(
        functools.partial(fused_kernel, rows, cols, heads, blocks),
        out_shape=[
            jax.ShapeDtypeStruct((heads, tokens_here, PAIR), half),
            jax.ShapeDtypeStruct((cols, blocks, BLOCK, PAIR), half),
        ],
        in_specs=[vmem] * 5 + [smem] * 3,
        out_specs=[vmem, vmem],
        scratch_shapes=scratch,
        compiler_params=pltpu.CompilerParams(collective_id=1, has_side_effects=True),
        name="head_attention",
    )(queries, key_rows, value_rows, out_grad, bits, partner, pick, shared_ids)


def unpack_kernel(groups, qa_ref, kvg_ref, att_ref, qg_ref, kg_ref, vg_ref):
    def split(pairs):
        left, right = pairs
        low = jnp.concatenate([left[:, :HEAD_DIM], right[:, :HEAD_DIM]], axis=1)
        high = jnp.concatenate([left[:, HEAD_DIM:], right[:, HEAD_DIM:]], axis=1)
        return low, high

    for p in range(qa_ref.shape[0] // 2):
        lanes = slice(p * PAIR, (p + 1) * PAIR)
        qg_ref[:, lanes], att_ref[:, lanes] = split([qa_ref[2 * p], qa_ref[2 * p + 1]])
        totals = []
        for side in range(2 * p, 2 * p + 2):
            total = kvg_ref[0, side]
            if groups > 1:
                total = total.astype(jnp.float32)
                for g in range(1, groups):
                    total = total + kvg_ref[g, side].astype(jnp.float32)
                total = total.astype(jnp.bfloat16)
            totals.append(total)
        kg_ref[:, lanes], vg_ref[:, lanes] = split(totals)


def unpack(qa, kvg):
    heads, tokens_here, _ = qa.shape
    groups = kvg.shape[0] // heads
    kvg = kvg.reshape(groups, heads, tokens_here, PAIR)
    rows = tokens_here // 2
    flat = pl.BlockSpec((rows, heads * HEAD_DIM), lambda t: (t, 0))
    shape = jax.ShapeDtypeStruct((tokens_here, heads * HEAD_DIM), jnp.bfloat16)
    return pl.pallas_call(
        functools.partial(unpack_kernel, groups),
        grid=(2,),
        in_specs=[
            pl.BlockSpec((heads, rows, PAIR), lambda t: (0, t, 0)),
            pl.BlockSpec((groups, heads, rows, PAIR), lambda t: (0, 0, t, 0)),
        ],
        out_specs=[flat] * 4,
        out_shape=[shape] * 4,
        name="unpack_heads",
    )(qa, kvg)


def body(queries, key_rows, value_rows, out_grad, dropout_bits, partner, block_pick, global_blocks):
    rows, cols = lax.axis_size("row"), lax.axis_size("col")
    qa, kvg = fused(
        rows, cols, queries, key_rows, value_rows, out_grad, dropout_bits, partner, block_pick, global_blocks
    )
    attended, query_grad, key_grad, value_grad = unpack(qa, kvg)
    return attended, query_grad, key_grad, value_grad


def solution(mesh):
    split = P(("row", "col"), None)
    return jax.shard_map(
        body,
        mesh=mesh,
        in_specs=(split,) * 5 + (P(),) * 3,
        out_specs=(split,) * 4,
        check_vma=False,
    )
```

```python
import functools

import jax
import jax.numpy as jnp
from jax import lax
from jax.experimental import pallas as pl
from jax.experimental.pallas import tpu as pltpu
from jax.sharding import PartitionSpec as P

HEAD_DIM = 64
BLOCK = 128
NGLOBAL = 2
NMATCH = 3
PAIR = 2 * HEAD_DIM

score_scale = 0.125
keep_scale = 1.0 / 0.9


def contract(a, b, dim_a, dim_b):
    return lax.dot_general(a, b, (((dim_a,), (dim_b,)), ((), ())), preferred_element_type=jnp.float32)


def stride_of(count):
    return max(1, count // 2 - 1)


def fused_kernel(
    rows, cols, heads, blocks,
    q_hbm, k_hbm, v_hbm, g_hbm, bits_hbm, partner_ref, pick_ref, global_ref,
    qa_land, kvg_land,
    q_ref, k_ref, v_ref, g_ref, bits_ref, kv_pack, qg_pack, kv_in, qg_in, bits_all, kv_ext, kv_turned, halo, shared, shared_turned,
    shared_keys, words_ref, s_ref, u_ref, p_ref, ds_ref, acc_ref, rand_ref, gacc_ref, halo_acc, gacc_in, qa_out, kvg_out, inverse_ref,
    kv_send, kv_recv, qg_send, qg_recv, bit_send, bit_recv, row_send, row_recv, back_send, back_recv, qa_send, qa_recv, kvg_send, kvg_recv, load_sems, own_sems,
):
    me, band = lax.axis_index("col"), lax.axis_index("row")
    head, group = me % heads, me // heads
    levels = heads.bit_length() - 1
    last = cols * blocks
    first = lax.broadcasted_iota(jnp.int32, (BLOCK, PAIR), 1) < HEAD_DIM
    zero = jnp.zeros((BLOCK, PAIR), jnp.bfloat16)

    load_k, load_v, load_bits, load_q, load_g = [
        pltpu.make_async_copy(source, target, load_sems.at[n])
        for n, (source, target) in enumerate(
            ((k_hbm, k_ref), (v_hbm, v_ref), (bits_hbm, bits_ref), (q_hbm, q_ref), (g_hbm, g_ref))
        )
    ]
    for load in (load_k, load_v, load_bits, load_q, load_g):
        load.start()
    barrier = pltpu.get_barrier_semaphore()

    def hello(step, carry):
        pl.semaphore_signal(barrier, inc=1, device_id={"col": (me + step) % cols})
        return carry

    lax.fori_loop(1, cols, hello, 0)
    for step in range(1, rows):
        pl.semaphore_signal(barrier, inc=1, device_id={"row": (band + step) % rows})

    load_k.wait()
    load_v.wait()
    for p in range(heads // 2):
        lanes = slice(p * PAIR, (p + 1) * PAIR)
        keys, values = k_ref[:, lanes], v_ref[:, lanes]
        left = jnp.concatenate([keys[:, :HEAD_DIM], values[:, :HEAD_DIM]], axis=1)
        right = jnp.concatenate([keys[:, HEAD_DIM:], values[:, HEAD_DIM:]], axis=1)
        kv_pack[2 * p] = left.reshape(blocks, BLOCK, PAIR)
        kv_pack[2 * p + 1] = right.reshape(blocks, BLOCK, PAIR)
    flags = [(me // 2 ** (levels - 1 - d)) % 2 for d in range(levels)]
    here = tuple(pl.ds(flag, 1) for flag in flags)
    load_bits.wait()
    for j in range(blocks):
        words = bits_ref[j * BLOCK : (j + 1) * BLOCK, :].astype(jnp.float32).T.astype(jnp.bfloat16)
        bits_all[here + (j,)] = words.reshape((1,) * levels + words.shape)

    pl.semaphore_wait(barrier, cols - 1 + rows - 1)

    def kv_copy(turn):
        step = (turn * stride_of(cols)) % cols
        other = (me + step) % cols
        return pltpu.make_async_remote_copy(
            src_ref=kv_pack.at[other % heads],
            dst_ref=kv_in.at[turn],
            send_sem=kv_send.at[step],
            recv_sem=kv_recv.at[step],
            device_id={"col": other},
        )

    def kv_start(turn, carry):
        kv_copy(turn).start()
        return carry

    bounds = [1 + (cols - 1) * i // levels for i in range(levels + 1)]

    def bits_copy(dim):
        bit = levels - 1 - dim
        region = (slice(None),) * dim + here[dim:]
        return pltpu.make_async_remote_copy(
            src_ref=bits_all.at[region],
            dst_ref=bits_all.at[region],
            send_sem=bit_send.at[dim],
            recv_sem=bit_recv.at[dim],
            device_id={"col": me + 2**bit - 2 * 2**bit * flags[dim]},
        )

    for dim in range(levels):
        copy = bits_copy(dim)
        copy.start()
        lax.fori_loop(bounds[dim], bounds[dim + 1], kv_start, 0)
        if dim == 0:
            load_q.wait()
            load_g.wait()
            for p in range(heads // 2):
                lanes = slice(p * PAIR, (p + 1) * PAIR)
                query = (q_ref[:, lanes].astype(jnp.float32) * score_scale).astype(jnp.bfloat16)
                grad = g_ref[:, lanes]
                qg_pack[2 * p] = jnp.concatenate([query[:, :HEAD_DIM], grad[:, :HEAD_DIM]], axis=1)
                qg_pack[2 * p + 1] = jnp.concatenate([query[:, HEAD_DIM:], grad[:, HEAD_DIM:]], axis=1)
        copy.wait()

    def qg_copy(turn):
        step = (turn * stride_of(heads)) % heads
        other = (head + step) % heads
        return pltpu.make_async_remote_copy(
            src_ref=qg_pack.at[other],
            dst_ref=qg_in.at[turn],
            send_sem=qg_send.at[step],
            recv_sem=qg_recv.at[step],
            device_id={"col": group * heads + other},
        )

    def qg_start(turn, carry):
        qg_copy(turn).start()
        return carry

    lax.fori_loop(1, heads, qg_start, 0)
    qg_in[0] = qg_pack[head]

    def find(place, carry):
        for r in range(NMATCH):
            def look(c, found):
                return found + jnp.where(partner_ref[r, band, c] == place, c, 0)

            inverse_ref[r, place] = jnp.minimum(lax.fori_loop(0, cols, look, 0), cols - 1)
        return carry

    lax.fori_loop(0, cols, find, 0)

    def clear(i, carry):
        acc_ref[i] = jnp.zeros((BLOCK, PAIR), jnp.float32)
        return carry

    lax.fori_loop(0, last + 2, clear, 0)
    gacc_ref[...] = jnp.zeros_like(gacc_ref)

    def turn_block(value):
        return value.astype(jnp.float32).T.astype(jnp.bfloat16)

    def place_kv(turn):
        source = (me + turn * (cols - stride_of(cols))) % cols
        for j in range(blocks):
            value = kv_in[turn, j]
            kv_ext[1 + source * blocks + j] = value
            kv_turned[1 + source * blocks + j] = turn_block(value)

    kv_in[0] = kv_pack[head]
    place_kv(0)

    def kv_take(turn, carry):
        kv_copy(turn).wait()
        place_kv(turn)
        return carry

    lax.fori_loop(1, cols, kv_take, 0)

    def edge_copies():
        return [
            pltpu.make_async_remote_copy(
                src_ref=kv_ext.at[last],
                dst_ref=halo.at[0],
                send_sem=row_send.at[0],
                recv_sem=row_recv.at[0],
                device_id={"row": (band + 1) % rows},
            ),
            pltpu.make_async_remote_copy(
                src_ref=kv_ext.at[1],
                dst_ref=halo.at[1],
                send_sem=row_send.at[1],
                recv_sem=row_recv.at[1],
                device_id={"row": (band + rows - 1) % rows},
            ),
        ]

    def shared_copy(step):
        return pltpu.make_async_remote_copy(
            src_ref=shared.at[band],
            dst_ref=shared.at[band],
            send_sem=row_send.at[1 + step],
            recv_sem=row_recv.at[1 + step],
            device_id={"row": (band + step) % rows},
        )

    for n in range(NGLOBAL):
        shared[band, n] = kv_ext[1 + jnp.clip(global_ref[n] - band * last, 0, last - 1)]
    for copy in edge_copies():
        copy.start()
    for step in range(1, rows):
        shared_copy(step).start()
    for copy in edge_copies():
        copy.wait()
    for side, place in ((0, 0), (1, last + 1)):
        value = halo[side]
        kv_ext[place] = value
        kv_turned[place] = turn_block(value)
    for step in range(1, rows):
        shared_copy(step).wait()
    for n in range(NGLOBAL):
        value = shared[global_ref[n] // last, n]
        shared_keys[n] = value
        shared_turned[n] = turn_block(value)

    for slot in range(heads):
        where_bits = tuple((slot // 2 ** (levels - 1 - d)) % 2 for d in range(levels))
        words_ref[slot] = bits_all[where_bits].astype(jnp.float32).astype(jnp.int32)

    wide = blocks * BLOCK
    reach = blocks + 2
    marks = jnp.left_shift(1, lax.broadcasted_iota(jnp.int32, (BLOCK // 8, 8, BLOCK), 1))
    p_ref[...] = jnp.zeros_like(p_ref)
    ds_ref[...] = jnp.zeros_like(ds_ref)
    first_all = lax.broadcasted_iota(jnp.int32, (wide, PAIR), 1) < HEAD_DIM
    zero_all = jnp.zeros((wide, PAIR), jnp.bfloat16)

    def attend(turn):
        slot = (head + turn * (heads - stride_of(heads))) % heads
        place = group * heads + slot
        far = [1 + partner_ref[r, band, place] * blocks + pick_ref[r, band, place] for r in range(NMATCH)]
        keys = [kv_ext[place * blocks + b] for b in range(reach)]
        keys += [shared_keys[n] for n in range(NGLOBAL)] + [kv_ext[b] for b in far]
        seen = [[(j, b - j) for j in range(blocks) if 0 <= b - j < 3] for b in range(reach)]
        seen += [[(j, 3 + f) for j in range(blocks)] for f in range(NGLOBAL + NMATCH)]
        packed = qg_in[turn]
        side_q = jnp.where(first_all, packed, zero_all)
        side_g = jnp.where(first_all, zero_all, packed)
        tops = [None] * blocks
        for b, pairs in enumerate(seen):
            lower, upper = pairs[0][0] * BLOCK, (pairs[-1][0] + 1) * BLOCK
            score = contract(keys[b], side_q[lower:upper], 1, 1)
            s_ref[b, :, lower:upper] = score
            for j, _ in pairs:
                tile = score[:, j * BLOCK - lower : (j + 1) * BLOCK - lower]
                part = jnp.max(tile.reshape(BLOCK // 8, 8, BLOCK), axis=0)
                tops[j] = part if tops[j] is None else jnp.maximum(tops[j], part)
        tops = [jnp.max(top, axis=0, keepdims=True) for top in tops]
        totals, mixed = [0.0] * blocks, [0.0] * blocks
        for b, pairs in enumerate(seen):
            lower, upper = pairs[0][0] * BLOCK, (pairs[-1][0] + 1) * BLOCK
            grad_p = contract(keys[b], side_g[lower:upper], 1, 1)
            for j, i in pairs:
                cols_j = slice(j * BLOCK, (j + 1) * BLOCK)
                words = words_ref[slot, j, i * BLOCK // 8 : (i + 1) * BLOCK // 8, :]
                keep = (jnp.broadcast_to(words[:, None, :], marks.shape) & marks) != 0
                weight = jnp.exp(s_ref[b, :, cols_j] - tops[j]).reshape(marks.shape)
                kept = jnp.where(keep, weight, 0.0)
                cross = kept * grad_p[:, j * BLOCK - lower : (j + 1) * BLOCK - lower].reshape(marks.shape)
                s_ref[b, :, cols_j] = weight.reshape(BLOCK, BLOCK)
                u_ref[b, :, cols_j] = cross.reshape(BLOCK, BLOCK)
                p_ref[b, :, cols_j] = kept.reshape(BLOCK, BLOCK).astype(jnp.bfloat16)
                totals[j] = totals[j] + jnp.sum(weight, axis=0)
                mixed[j] = mixed[j] + jnp.sum(cross, axis=0)
        scales, deltas = [], []
        for j in range(blocks):
            inverse = 1.0 / jnp.sum(totals[j], axis=0, keepdims=True)
            deltas.append(jnp.sum(mixed[j], axis=0, keepdims=True) * inverse)
            scales.append(inverse * keep_scale)
        for b, pairs in enumerate(seen):
            for j, _ in pairs:
                cols_j = slice(j * BLOCK, (j + 1) * BLOCK)
                ds_ref[b, :, cols_j] = (u_ref[b, :, cols_j] - s_ref[b, :, cols_j] * deltas[j]).astype(jnp.bfloat16)
        turned = [kv_turned[place * blocks + b] for b in range(reach)]
        turned += [shared_turned[n] for n in range(NGLOBAL)] + [kv_turned[b] for b in far]
        turned = jnp.concatenate(turned, axis=1)
        whole = (reach + NGLOBAL + NMATCH) * BLOCK
        out_p = contract(turned, p_ref[...].reshape(whole, wide), 1, 0)
        out_s = contract(turned, ds_ref[...].reshape(whole, wide), 1, 0)
        factors = []
        for j in range(blocks):
            cols_j = slice(j * BLOCK, (j + 1) * BLOCK)
            out = jnp.concatenate(
                [out_s[:HEAD_DIM, cols_j] * (scales[j] * score_scale), out_p[HEAD_DIM:, cols_j] * scales[j]], axis=0
            )
            qa_out[turn, cols_j, :] = out.T.astype(jnp.bfloat16)
            factors.append(jnp.broadcast_to(scales[j], (BLOCK, BLOCK)).T)
        scaled = (packed.astype(jnp.float32) * jnp.concatenate(factors, axis=0)).astype(jnp.bfloat16)
        grads = contract(ds_ref[...].reshape(whole, wide), jnp.where(first_all, scaled, zero_all), 1, 0)
        grads = grads + contract(p_ref[...].reshape(whole, wide), jnp.where(first_all, zero_all, scaled), 1, 0)
        for b in range(reach):
            acc_ref[place * blocks + b] += grads[b * BLOCK : (b + 1) * BLOCK]
        base = reach * BLOCK
        for n in range(NGLOBAL):
            gacc_ref[n] += grads[base + n * BLOCK : base + (n + 1) * BLOCK]
        base += NGLOBAL * BLOCK
        for r in range(NMATCH):
            rand_ref[slot, r] = grads[base + r * BLOCK : base + (r + 1) * BLOCK]

    def qa_copy(turn):
        step = (turn * stride_of(heads)) % heads
        slot = (head - step + heads) % heads
        return pltpu.make_async_remote_copy(
            src_ref=qa_out.at[turn],
            dst_ref=qa_land.at[head],
            send_sem=qa_send.at[step],
            recv_sem=qa_recv.at[step],
            device_id={"col": group * heads + slot},
        )

    def segment(turn, carry):
        qg_copy(turn).wait()
        attend(turn)
        qa_copy(turn).start()
        return carry

    attend(0)
    lax.fori_loop(1, heads, segment, 0)
    own_qa = pltpu.make_async_copy(qa_out.at[0], qa_land.at[head], own_sems.at[0])
    own_qa.start()

    def back_copies():
        copies = [
            pltpu.make_async_remote_copy(
                src_ref=acc_ref.at[last + 1],
                dst_ref=halo_acc.at[0],
                send_sem=back_send.at[0],
                recv_sem=back_recv.at[0],
                device_id={"row": (band + 1) % rows},
            ),
            pltpu.make_async_remote_copy(
                src_ref=acc_ref.at[0],
                dst_ref=halo_acc.at[1],
                send_sem=back_send.at[1],
                recv_sem=back_recv.at[1],
                device_id={"row": (band + rows - 1) % rows},
            ),
        ]
        for step in range(1, rows):
            copies.append(
                pltpu.make_async_remote_copy(
                    src_ref=gacc_ref,
                    dst_ref=gacc_in.at[band],
                    send_sem=back_send.at[1 + step],
                    recv_sem=back_recv.at[1 + step],
                    device_id={"row": (band + step) % rows},
                )
            )
        return copies

    for copy in back_copies():
        copy.start()
    for copy in back_copies():
        copy.wait()
    sums = []
    for n in range(NGLOBAL):
        total = gacc_ref[n]
        for step in range(1, rows):
            total = total + gacc_in[(band + step) % rows, n]
        s_ref[n, :, :BLOCK] = total
    acc_ref[1] += halo_acc[0]
    acc_ref[last] += halo_acc[1]

    def collect(turn):
        place = (me + turn * stride_of(cols)) % cols
        totals = [acc_ref[1 + place * blocks + j] for j in range(blocks)]
        for r in range(NMATCH):
            source = inverse_ref[r, place]
            chosen = jnp.where(source // heads == group, pick_ref[r, band, source], blocks)
            part = rand_ref[source % heads, r]
            totals = [total + jnp.where(chosen == j, part, 0.0) for j, total in enumerate(totals)]
        for n in range(NGLOBAL):
            chosen = global_ref[n] - (band * cols + place) * blocks
            part = s_ref[n, :, :BLOCK]
            totals = [total + jnp.where(chosen == j, part, 0.0) for j, total in enumerate(totals)]
        for j in range(blocks):
            kvg_out[turn, j] = totals[j].astype(jnp.bfloat16)

    def kvg_copy(turn):
        step = (turn * stride_of(cols)) % cols
        other = (me + step) % cols
        return pltpu.make_async_remote_copy(
            src_ref=kvg_out.at[turn],
            dst_ref=kvg_land.at[me],
            send_sem=kvg_send.at[step],
            recv_sem=kvg_recv.at[step],
            device_id={"col": other},
        )

    def give(turn, carry):
        collect(turn)
        kvg_copy(turn).start()
        return carry

    lax.fori_loop(1, cols, give, 0)
    collect(0)
    own_kvg = pltpu.make_async_copy(kvg_out.at[0], kvg_land.at[me], own_sems.at[1])
    own_kvg.start()

    def qa_finish(turn, carry):
        qa_copy(turn).wait()
        return carry

    lax.fori_loop(1, heads, qa_finish, 0)

    def kvg_finish(turn, carry):
        kvg_copy(turn).wait()
        return carry

    lax.fori_loop(1, cols, kvg_finish, 0)
    own_qa.wait()
    own_kvg.wait()


def fused(rows, cols, queries, key_rows, value_rows, out_grad, bits, partner, pick, shared_ids):
    tokens_here, width = queries.shape
    blocks = tokens_here // BLOCK
    heads = width // HEAD_DIM
    levels = heads.bit_length() - 1
    last = cols * blocks
    tiles = blocks + 2 + NGLOBAL + NMATCH
    half, full = jnp.bfloat16, jnp.float32
    anywhere = pl.BlockSpec(memory_space=pl.ANY)
    smem = pl.BlockSpec(memory_space=pltpu.SMEM)

    scratch = [pltpu.VMEM((tokens_here, width), half)] * 4 + [pltpu.VMEM(bits.shape, bits.dtype)]
    scratch += [
        pltpu.VMEM((heads, blocks, BLOCK, PAIR), half),
        pltpu.VMEM((heads, tokens_here, PAIR), half),
        pltpu.VMEM((cols, blocks, BLOCK, PAIR), half),
        pltpu.VMEM((heads, tokens_here, PAIR), half),
        pltpu.VMEM((2,) * levels + (blocks, BLOCK, BLOCK), half),
        pltpu.VMEM((last + 2, BLOCK, PAIR), half),
        pltpu.VMEM((last + 2, PAIR, BLOCK), half),
        pltpu.VMEM((2, BLOCK, PAIR), half),
        pltpu.VMEM((rows, NGLOBAL, BLOCK, PAIR), half),
        pltpu.VMEM((NGLOBAL, PAIR, BLOCK), half),
        pltpu.VMEM((NGLOBAL, BLOCK, PAIR), half),
        pltpu.VMEM((heads, blocks, BLOCK, BLOCK), jnp.int32),
        pltpu.VMEM((tiles, BLOCK, tokens_here), full),
        pltpu.VMEM((tiles, BLOCK, tokens_here), full),
        pltpu.VMEM((tiles, BLOCK, tokens_here), half),
        pltpu.VMEM((tiles, BLOCK, tokens_here), half),
        pltpu.VMEM((last + 2, BLOCK, PAIR), full),
        pltpu.VMEM((heads, NMATCH, BLOCK, PAIR), full),
        pltpu.VMEM((NGLOBAL, BLOCK, PAIR), full),
        pltpu.VMEM((2, BLOCK, PAIR), full),
        pltpu.VMEM((rows, NGLOBAL, BLOCK, PAIR), full),
        pltpu.VMEM((heads, tokens_here, PAIR), half),
        pltpu.VMEM((cols, blocks, BLOCK, PAIR), half),
        pltpu.SMEM((NMATCH, cols), jnp.int32),
    ]
    for count in (cols, heads, levels, rows + 1, rows + 1, heads, cols):
        scratch += [pltpu.SemaphoreType.DMA((count,))] * 2
    scratch += [pltpu.SemaphoreType.DMA((5,)), pltpu.SemaphoreType.DMA((2,))]
    return pl.pallas_call(
        functools.partial(fused_kernel, rows, cols, heads, blocks),
        out_shape=[
            jax.ShapeDtypeStruct((heads, tokens_here, PAIR), half),
            jax.ShapeDtypeStruct((cols, blocks, BLOCK, PAIR), half),
        ],
        in_specs=[anywhere] * 5 + [smem] * 3,
        out_specs=[anywhere, anywhere],
        scratch_shapes=scratch,
        compiler_params=pltpu.CompilerParams(collective_id=1, has_side_effects=True),
        name="head_attention",
    )(queries, key_rows, value_rows, out_grad, bits, partner, pick, shared_ids)


def unpack_kernel(groups, qa_ref, kvg_ref, att_ref, qg_ref, kg_ref, vg_ref):
    def split(pairs):
        left, right = pairs
        low = jnp.concatenate([left[:, :HEAD_DIM], right[:, :HEAD_DIM]], axis=1)
        high = jnp.concatenate([left[:, HEAD_DIM:], right[:, HEAD_DIM:]], axis=1)
        return low, high

    for p in range(qa_ref.shape[0] // 2):
        lanes = slice(p * PAIR, (p + 1) * PAIR)
        qg_ref[:, lanes], att_ref[:, lanes] = split([qa_ref[2 * p], qa_ref[2 * p + 1]])
        totals = []
        for side in range(2 * p, 2 * p + 2):
            total = kvg_ref[0, side]
            if groups > 1:
                total = total.astype(jnp.float32)
                for g in range(1, groups):
                    total = total + kvg_ref[g, side].astype(jnp.float32)
                total = total.astype(jnp.bfloat16)
            totals.append(total)
        kg_ref[:, lanes], vg_ref[:, lanes] = split(totals)


def unpack(qa, kvg):
    heads, tokens_here, _ = qa.shape
    groups = kvg.shape[0] // heads
    kvg = kvg.reshape(groups, heads, tokens_here, PAIR)
    rows = tokens_here // 2
    flat = pl.BlockSpec((rows, heads * HEAD_DIM), lambda t: (t, 0))
    shape = jax.ShapeDtypeStruct((tokens_here, heads * HEAD_DIM), jnp.bfloat16)
    return pl.pallas_call(
        functools.partial(unpack_kernel, groups),
        grid=(2,),
        in_specs=[
            pl.BlockSpec((heads, rows, PAIR), lambda t: (0, t, 0)),
            pl.BlockSpec((groups, heads, rows, PAIR), lambda t: (0, 0, t, 0)),
        ],
        out_specs=[flat] * 4,
        out_shape=[shape] * 4,
        name="unpack_heads",
    )(qa, kvg)


def body(queries, key_rows, value_rows, out_grad, dropout_bits, partner, block_pick, global_blocks):
    rows, cols = lax.axis_size("row"), lax.axis_size("col")
    qa, kvg = fused(
        rows, cols, queries, key_rows, value_rows, out_grad, dropout_bits, partner, block_pick, global_blocks
    )
    attended, query_grad, key_grad, value_grad = unpack(qa, kvg)
    return attended, query_grad, key_grad, value_grad


def solution(mesh):
    split = P(("row", "col"), None)
    return jax.shard_map(
        body,
        mesh=mesh,
        in_specs=(split,) * 5 + (P(),) * 3,
        out_specs=(split,) * 4,
        check_vma=False,
    )
```

```python
import functools

import jax
import jax.numpy as jnp
from jax import lax
from jax.experimental import pallas as pl
from jax.experimental.pallas import tpu as pltpu
from jax.sharding import PartitionSpec as P

HEAD_DIM = 64
BLOCK = 128
NGLOBAL = 2
NMATCH = 3
PAIR = 2 * HEAD_DIM

score_scale = 0.125
keep_scale = 1.0 / 0.9


def contract(a, b, dim_a, dim_b):
    return lax.dot_general(a, b, (((dim_a,), (dim_b,)), ((), ())), preferred_element_type=jnp.float32)


def stride_of(count):
    return max(1, count // 2 - 1)


def fused_kernel(
    rows, cols, heads, blocks,
    q_hbm, k_hbm, v_hbm, g_hbm, bits_hbm, partner_ref, pick_ref, global_ref,
    qa_land, kvg_land,
    q_ref, k_ref, v_ref, g_ref, bits_ref, kv_pack, qg_pack, kv_in, qg_in, bits_all, kv_ext, kv_turned, halo, shared, shared_turned,
    shared_keys, words_ref, s_ref, u_ref, p_ref, ds_ref, acc_ref, rand_ref, gacc_ref, halo_acc, gacc_in, qa_out, kvg_out, inverse_ref,
    kv_send, kv_recv, qg_send, qg_recv, bit_send, bit_recv, row_send, row_recv, back_send, back_recv, qa_send, qa_recv, kvg_send, kvg_recv, load_sems, own_sems,
):
    me, band = lax.axis_index("col"), lax.axis_index("row")
    head, group = me % heads, me // heads
    levels = heads.bit_length() - 1
    last = cols * blocks
    first = lax.broadcasted_iota(jnp.int32, (BLOCK, PAIR), 1) < HEAD_DIM
    zero = jnp.zeros((BLOCK, PAIR), jnp.bfloat16)

    load_k, load_v, load_bits, load_q, load_g = [
        pltpu.make_async_copy(source, target, load_sems.at[n])
        for n, (source, target) in enumerate(
            ((k_hbm, k_ref), (v_hbm, v_ref), (bits_hbm, bits_ref), (q_hbm, q_ref), (g_hbm, g_ref))
        )
    ]
    for load in (load_k, load_v, load_bits, load_q, load_g):
        load.start()
    barrier = pltpu.get_barrier_semaphore()

    def hello(step, carry):
        pl.semaphore_signal(barrier, inc=1, device_id={"col": (me + step) % cols})
        return carry

    lax.fori_loop(1, cols, hello, 0)
    for step in range(1, rows):
        pl.semaphore_signal(barrier, inc=1, device_id={"row": (band + step) % rows})

    load_k.wait()
    load_v.wait()
    for p in range(heads // 2):
        lanes = slice(p * PAIR, (p + 1) * PAIR)
        keys, values = k_ref[:, lanes], v_ref[:, lanes]
        left = jnp.concatenate([keys[:, :HEAD_DIM], values[:, :HEAD_DIM]], axis=1)
        right = jnp.concatenate([keys[:, HEAD_DIM:], values[:, HEAD_DIM:]], axis=1)
        kv_pack[2 * p] = left.reshape(blocks, BLOCK, PAIR)
        kv_pack[2 * p + 1] = right.reshape(blocks, BLOCK, PAIR)
    flags = [(me // 2 ** (levels - 1 - d)) % 2 for d in range(levels)]
    here = tuple(pl.ds(flag, 1) for flag in flags)
    load_bits.wait()
    for j in range(blocks):
        words = bits_ref[j * BLOCK : (j + 1) * BLOCK, :].astype(jnp.float32).T.astype(jnp.bfloat16)
        bits_all[here + (j,)] = words.reshape((1,) * levels + words.shape)

    pl.semaphore_wait(barrier, cols - 1 + rows - 1)

    def kv_copy(turn):
        step = (turn * stride_of(cols)) % cols
        other = (me + step) % cols
        return pltpu.make_async_remote_copy(
            src_ref=kv_pack.at[other % heads],
            dst_ref=kv_in.at[turn],
            send_sem=kv_send.at[step],
            recv_sem=kv_recv.at[step],
            device_id={"col": other},
        )

    def kv_start(turn, carry):
        kv_copy(turn).start()
        return carry

    bounds = [1 + (cols - 1) * i // levels for i in range(levels + 1)]

    def bits_copy(dim):
        bit = levels - 1 - dim
        region = (slice(None),) * dim + here[dim:]
        return pltpu.make_async_remote_copy(
            src_ref=bits_all.at[region],
            dst_ref=bits_all.at[region],
            send_sem=bit_send.at[dim],
            recv_sem=bit_recv.at[dim],
            device_id={"col": me + 2**bit - 2 * 2**bit * flags[dim]},
        )

    for dim in range(levels):
        copy = bits_copy(dim)
        copy.start()
        lax.fori_loop(bounds[dim], bounds[dim + 1], kv_start, 0)
        if dim == 0:
            load_q.wait()
            load_g.wait()
            for p in range(heads // 2):
                lanes = slice(p * PAIR, (p + 1) * PAIR)
                query = (q_ref[:, lanes].astype(jnp.float32) * score_scale).astype(jnp.bfloat16)
                grad = g_ref[:, lanes]
                qg_pack[2 * p] = jnp.concatenate([query[:, :HEAD_DIM], grad[:, :HEAD_DIM]], axis=1)
                qg_pack[2 * p + 1] = jnp.concatenate([query[:, HEAD_DIM:], grad[:, HEAD_DIM:]], axis=1)
        copy.wait()

    def qg_copy(turn):
        step = (turn * stride_of(heads)) % heads
        other = (head + step) % heads
        return pltpu.make_async_remote_copy(
            src_ref=qg_pack.at[other],
            dst_ref=qg_in.at[turn],
            send_sem=qg_send.at[step],
            recv_sem=qg_recv.at[step],
            device_id={"col": group * heads + other},
        )

    def qg_start(turn, carry):
        qg_copy(turn).start()
        return carry

    lax.fori_loop(1, heads, qg_start, 0)
    qg_in[0] = qg_pack[head]

    def find(place, carry):
        for r in range(NMATCH):
            def look(c, found):
                return found + jnp.where(partner_ref[r, band, c] == place, c, 0)

            inverse_ref[r, place] = jnp.minimum(lax.fori_loop(0, cols, look, 0), cols - 1)
        return carry

    lax.fori_loop(0, cols, find, 0)

    def clear(i, carry):
        acc_ref[i] = jnp.zeros((BLOCK, PAIR), jnp.float32)
        return carry

    lax.fori_loop(0, last + 2, clear, 0)
    gacc_ref[...] = jnp.zeros_like(gacc_ref)
    p_ref[...] = jnp.zeros_like(p_ref)
    ds_ref[...] = jnp.zeros_like(ds_ref)
    for slot in range(heads):
        where_bits = tuple((slot // 2 ** (levels - 1 - d)) % 2 for d in range(levels))
        words_ref[slot] = bits_all[where_bits].astype(jnp.float32).astype(jnp.int32)


    def turn_block(value):
        return value.astype(jnp.float32).T.astype(jnp.bfloat16)

    def place_kv(turn):
        source = (me + turn * (cols - stride_of(cols))) % cols
        for j in range(blocks):
            value = kv_in[turn, j]
            kv_ext[1 + source * blocks + j] = value
            kv_turned[1 + source * blocks + j] = turn_block(value)

    kv_in[0] = kv_pack[head]
    place_kv(0)

    def kv_take(turn, carry):
        kv_copy(turn).wait()
        place_kv(turn)
        return carry

    lax.fori_loop(1, cols, kv_take, 0)

    def edge_copies():
        return [
            pltpu.make_async_remote_copy(
                src_ref=kv_ext.at[last],
                dst_ref=halo.at[0],
                send_sem=row_send.at[0],
                recv_sem=row_recv.at[0],
                device_id={"row": (band + 1) % rows},
            ),
            pltpu.make_async_remote_copy(
                src_ref=kv_ext.at[1],
                dst_ref=halo.at[1],
                send_sem=row_send.at[1],
                recv_sem=row_recv.at[1],
                device_id={"row": (band + rows - 1) % rows},
            ),
        ]

    def shared_copy(step):
        return pltpu.make_async_remote_copy(
            src_ref=shared.at[band],
            dst_ref=shared.at[band],
            send_sem=row_send.at[1 + step],
            recv_sem=row_recv.at[1 + step],
            device_id={"row": (band + step) % rows},
        )

    for n in range(NGLOBAL):
        shared[band, n] = kv_ext[1 + jnp.clip(global_ref[n] - band * last, 0, last - 1)]
    for copy in edge_copies():
        copy.start()
    for step in range(1, rows):
        shared_copy(step).start()
    for copy in edge_copies():
        copy.wait()
    for side, place in ((0, 0), (1, last + 1)):
        value = halo[side]
        kv_ext[place] = value
        kv_turned[place] = turn_block(value)
    for step in range(1, rows):
        shared_copy(step).wait()
    for n in range(NGLOBAL):
        value = shared[global_ref[n] // last, n]
        shared_keys[n] = value
        shared_turned[n] = turn_block(value)

    wide = blocks * BLOCK
    reach = blocks + 2
    marks = jnp.left_shift(1, lax.broadcasted_iota(jnp.int32, (BLOCK // 8, 8, BLOCK), 1))
    first_all = lax.broadcasted_iota(jnp.int32, (wide, PAIR), 1) < HEAD_DIM
    zero_all = jnp.zeros((wide, PAIR), jnp.bfloat16)

    def attend(turn):
        slot = (head + turn * (heads - stride_of(heads))) % heads
        place = group * heads + slot
        far = [1 + partner_ref[r, band, place] * blocks + pick_ref[r, band, place] for r in range(NMATCH)]
        keys = [kv_ext[place * blocks + b] for b in range(reach)]
        keys += [shared_keys[n] for n in range(NGLOBAL)] + [kv_ext[b] for b in far]
        seen = [[(j, b - j) for j in range(blocks) if 0 <= b - j < 3] for b in range(reach)]
        seen += [[(j, 3 + f) for j in range(blocks)] for f in range(NGLOBAL + NMATCH)]
        packed = qg_in[turn]
        side_q = jnp.where(first_all, packed, zero_all)
        side_g = jnp.where(first_all, zero_all, packed)
        tops = [None] * blocks
        for b, pairs in enumerate(seen):
            lower, upper = pairs[0][0] * BLOCK, (pairs[-1][0] + 1) * BLOCK
            score = contract(keys[b], side_q[lower:upper], 1, 1)
            s_ref[b, :, lower:upper] = score
            for j, _ in pairs:
                tile = score[:, j * BLOCK - lower : (j + 1) * BLOCK - lower]
                part = jnp.max(tile.reshape(BLOCK // 8, 8, BLOCK), axis=0)
                tops[j] = part if tops[j] is None else jnp.maximum(tops[j], part)
        tops = [jnp.max(top, axis=0, keepdims=True) for top in tops]
        totals, mixed = [0.0] * blocks, [0.0] * blocks
        for b, pairs in enumerate(seen):
            lower, upper = pairs[0][0] * BLOCK, (pairs[-1][0] + 1) * BLOCK
            grad_p = contract(keys[b], side_g[lower:upper], 1, 1)
            for j, i in pairs:
                cols_j = slice(j * BLOCK, (j + 1) * BLOCK)
                words = words_ref[slot, j, i * BLOCK // 8 : (i + 1) * BLOCK // 8, :]
                keep = (jnp.broadcast_to(words[:, None, :], marks.shape) & marks) != 0
                weight = jnp.exp(s_ref[b, :, cols_j] - tops[j]).reshape(marks.shape)
                kept = jnp.where(keep, weight, 0.0)
                cross = kept * grad_p[:, j * BLOCK - lower : (j + 1) * BLOCK - lower].reshape(marks.shape)
                s_ref[b, :, cols_j] = weight.reshape(BLOCK, BLOCK)
                u_ref[b, :, cols_j] = cross.reshape(BLOCK, BLOCK)
                p_ref[b, :, cols_j] = kept.reshape(BLOCK, BLOCK).astype(jnp.bfloat16)
                totals[j] = totals[j] + jnp.sum(weight, axis=0)
                mixed[j] = mixed[j] + jnp.sum(cross, axis=0)
        scales, deltas = [], []
        for j in range(blocks):
            inverse = 1.0 / jnp.sum(totals[j], axis=0, keepdims=True)
            deltas.append(jnp.sum(mixed[j], axis=0, keepdims=True) * inverse)
            scales.append(inverse * keep_scale)
        turned = [kv_turned[place * blocks + b] for b in range(reach)]
        turned += [shared_turned[n] for n in range(NGLOBAL)] + [kv_turned[b] for b in far]
        turned = jnp.concatenate(turned, axis=1)
        whole = (reach + NGLOBAL + NMATCH) * BLOCK
        out_p = contract(turned, p_ref[...].reshape(whole, wide), 1, 0)
        factors = jnp.concatenate([jnp.broadcast_to(scales[j], (BLOCK, BLOCK)).T for j in range(blocks)], axis=0)
        scaled = (packed.astype(jnp.float32) * factors).astype(jnp.bfloat16)

        def gather(grads):
            for b in range(reach):
                acc_ref[place * blocks + b] += grads[b * BLOCK : (b + 1) * BLOCK]
            base = reach * BLOCK
            for n in range(NGLOBAL):
                gacc_ref[n] += grads[base + n * BLOCK : base + (n + 1) * BLOCK]
            base += NGLOBAL * BLOCK
            return [grads[base + r * BLOCK : base + (r + 1) * BLOCK] for r in range(NMATCH)]

        picked = gather(contract(p_ref[...].reshape(whole, wide), jnp.where(first_all, zero_all, scaled), 1, 0))
        for r in range(NMATCH):
            rand_ref[slot, r] = picked[r]
        for b, pairs in enumerate(seen):
            for j, _ in pairs:
                cols_j = slice(j * BLOCK, (j + 1) * BLOCK)
                ds_ref[b, :, cols_j] = (u_ref[b, :, cols_j] - s_ref[b, :, cols_j] * deltas[j]).astype(jnp.bfloat16)
        out_s = contract(turned, ds_ref[...].reshape(whole, wide), 1, 0)
        for j in range(blocks):
            cols_j = slice(j * BLOCK, (j + 1) * BLOCK)
            out = jnp.concatenate(
                [out_s[:HEAD_DIM, cols_j] * (scales[j] * score_scale), out_p[HEAD_DIM:, cols_j] * scales[j]], axis=0
            )
            qa_out[turn, cols_j, :] = out.T.astype(jnp.bfloat16)
        picked = gather(contract(ds_ref[...].reshape(whole, wide), jnp.where(first_all, scaled, zero_all), 1, 0))
        for r in range(NMATCH):
            rand_ref[slot, r] += picked[r]

    def qa_copy(turn):
        step = (turn * stride_of(heads)) % heads
        slot = (head - step + heads) % heads
        return pltpu.make_async_remote_copy(
            src_ref=qa_out.at[turn],
            dst_ref=qa_land.at[head],
            send_sem=qa_send.at[step],
            recv_sem=qa_recv.at[step],
            device_id={"col": group * heads + slot},
        )

    def segment(turn, carry):
        qg_copy(turn).wait()
        attend(turn)
        qa_copy(turn).start()
        return carry

    attend(0)
    lax.fori_loop(1, heads, segment, 0)
    own_qa = pltpu.make_async_copy(qa_out.at[0], qa_land.at[head], own_sems.at[0])
    own_qa.start()

    def back_copies():
        copies = [
            pltpu.make_async_remote_copy(
                src_ref=acc_ref.at[last + 1],
                dst_ref=halo_acc.at[0],
                send_sem=back_send.at[0],
                recv_sem=back_recv.at[0],
                device_id={"row": (band + 1) % rows},
            ),
            pltpu.make_async_remote_copy(
                src_ref=acc_ref.at[0],
                dst_ref=halo_acc.at[1],
                send_sem=back_send.at[1],
                recv_sem=back_recv.at[1],
                device_id={"row": (band + rows - 1) % rows},
            ),
        ]
        for step in range(1, rows):
            copies.append(
                pltpu.make_async_remote_copy(
                    src_ref=gacc_ref,
                    dst_ref=gacc_in.at[band],
                    send_sem=back_send.at[1 + step],
                    recv_sem=back_recv.at[1 + step],
                    device_id={"row": (band + step) % rows},
                )
            )
        return copies

    for copy in back_copies():
        copy.start()
    for copy in back_copies():
        copy.wait()
    sums = []
    for n in range(NGLOBAL):
        total = gacc_ref[n]
        for step in range(1, rows):
            total = total + gacc_in[(band + step) % rows, n]
        s_ref[n, :, :BLOCK] = total
    acc_ref[1] += halo_acc[0]
    acc_ref[last] += halo_acc[1]

    def collect(turn):
        place = (me + turn * stride_of(cols)) % cols
        totals = [acc_ref[1 + place * blocks + j] for j in range(blocks)]
        for r in range(NMATCH):
            source = inverse_ref[r, place]
            chosen = jnp.where(source // heads == group, pick_ref[r, band, source], blocks)
            part = rand_ref[source % heads, r]
            totals = [total + jnp.where(chosen == j, part, 0.0) for j, total in enumerate(totals)]
        for n in range(NGLOBAL):
            chosen = global_ref[n] - (band * cols + place) * blocks
            part = s_ref[n, :, :BLOCK]
            totals = [total + jnp.where(chosen == j, part, 0.0) for j, total in enumerate(totals)]
        for j in range(blocks):
            kvg_out[turn, j] = totals[j].astype(jnp.bfloat16)

    def kvg_copy(turn):
        step = (turn * stride_of(cols)) % cols
        other = (me + step) % cols
        return pltpu.make_async_remote_copy(
            src_ref=kvg_out.at[turn],
            dst_ref=kvg_land.at[me],
            send_sem=kvg_send.at[step],
            recv_sem=kvg_recv.at[step],
            device_id={"col": other},
        )

    def give(turn, carry):
        collect(turn)
        kvg_copy(turn).start()
        return carry

    lax.fori_loop(1, cols, give, 0)
    collect(0)
    own_kvg = pltpu.make_async_copy(kvg_out.at[0], kvg_land.at[me], own_sems.at[1])
    own_kvg.start()

    def qa_finish(turn, carry):
        qa_copy(turn).wait()
        return carry

    lax.fori_loop(1, heads, qa_finish, 0)

    def kvg_finish(turn, carry):
        kvg_copy(turn).wait()
        return carry

    lax.fori_loop(1, cols, kvg_finish, 0)
    own_qa.wait()
    own_kvg.wait()


def fused(rows, cols, queries, key_rows, value_rows, out_grad, bits, partner, pick, shared_ids):
    tokens_here, width = queries.shape
    blocks = tokens_here // BLOCK
    heads = width // HEAD_DIM
    levels = heads.bit_length() - 1
    last = cols * blocks
    tiles = blocks + 2 + NGLOBAL + NMATCH
    half, full = jnp.bfloat16, jnp.float32
    anywhere = pl.BlockSpec(memory_space=pl.ANY)
    smem = pl.BlockSpec(memory_space=pltpu.SMEM)

    scratch = [pltpu.VMEM((tokens_here, width), half)] * 4 + [pltpu.VMEM(bits.shape, bits.dtype)]
    scratch += [
        pltpu.VMEM((heads, blocks, BLOCK, PAIR), half),
        pltpu.VMEM((heads, tokens_here, PAIR), half),
        pltpu.VMEM((cols, blocks, BLOCK, PAIR), half),
        pltpu.VMEM((heads, tokens_here, PAIR), half),
        pltpu.VMEM((2,) * levels + (blocks, BLOCK, BLOCK), half),
        pltpu.VMEM((last + 2, BLOCK, PAIR), half),
        pltpu.VMEM((last + 2, PAIR, BLOCK), half),
        pltpu.VMEM((2, BLOCK, PAIR), half),
        pltpu.VMEM((rows, NGLOBAL, BLOCK, PAIR), half),
        pltpu.VMEM((NGLOBAL, PAIR, BLOCK), half),
        pltpu.VMEM((NGLOBAL, BLOCK, PAIR), half),
        pltpu.VMEM((heads, blocks, BLOCK, BLOCK), jnp.int32),
        pltpu.VMEM((tiles, BLOCK, tokens_here), full),
        pltpu.VMEM((tiles, BLOCK, tokens_here), full),
        pltpu.VMEM((tiles, BLOCK, tokens_here), half),
        pltpu.VMEM((tiles, BLOCK, tokens_here), half),
        pltpu.VMEM((last + 2, BLOCK, PAIR), full),
        pltpu.VMEM((heads, NMATCH, BLOCK, PAIR), full),
        pltpu.VMEM((NGLOBAL, BLOCK, PAIR), full),
        pltpu.VMEM((2, BLOCK, PAIR), full),
        pltpu.VMEM((rows, NGLOBAL, BLOCK, PAIR), full),
        pltpu.VMEM((heads, tokens_here, PAIR), half),
        pltpu.VMEM((cols, blocks, BLOCK, PAIR), half),
        pltpu.SMEM((NMATCH, cols), jnp.int32),
    ]
    for count in (cols, heads, levels, rows + 1, rows + 1, heads, cols):
        scratch += [pltpu.SemaphoreType.DMA((count,))] * 2
    scratch += [pltpu.SemaphoreType.DMA((5,)), pltpu.SemaphoreType.DMA((2,))]
    return pl.pallas_call(
        functools.partial(fused_kernel, rows, cols, heads, blocks),
        out_shape=[
            jax.ShapeDtypeStruct((heads, tokens_here, PAIR), half),
            jax.ShapeDtypeStruct((cols, blocks, BLOCK, PAIR), half),
        ],
        in_specs=[anywhere] * 5 + [smem] * 3,
        out_specs=[anywhere, anywhere],
        scratch_shapes=scratch,
        compiler_params=pltpu.CompilerParams(collective_id=1, has_side_effects=True),
        name="head_attention",
    )(queries, key_rows, value_rows, out_grad, bits, partner, pick, shared_ids)


def unpack_kernel(groups, qa_ref, kvg_ref, att_ref, qg_ref, kg_ref, vg_ref):
    def split(pairs):
        left, right = pairs
        low = jnp.concatenate([left[:, :HEAD_DIM], right[:, :HEAD_DIM]], axis=1)
        high = jnp.concatenate([left[:, HEAD_DIM:], right[:, HEAD_DIM:]], axis=1)
        return low, high

    for p in range(qa_ref.shape[0] // 2):
        lanes = slice(p * PAIR, (p + 1) * PAIR)
        qg_ref[:, lanes], att_ref[:, lanes] = split([qa_ref[2 * p], qa_ref[2 * p + 1]])
        totals = []
        for side in range(2 * p, 2 * p + 2):
            total = kvg_ref[0, side]
            if groups > 1:
                total = total.astype(jnp.float32)
                for g in range(1, groups):
                    total = total + kvg_ref[g, side].astype(jnp.float32)
                total = total.astype(jnp.bfloat16)
            totals.append(total)
        kg_ref[:, lanes], vg_ref[:, lanes] = split(totals)


def unpack(qa, kvg):
    heads, tokens_here, _ = qa.shape
    groups = kvg.shape[0] // heads
    kvg = kvg.reshape(groups, heads, tokens_here, PAIR)
    rows = tokens_here // 2
    flat = pl.BlockSpec((rows, heads * HEAD_DIM), lambda t: (t, 0))
    shape = jax.ShapeDtypeStruct((tokens_here, heads * HEAD_DIM), jnp.bfloat16)
    return pl.pallas_call(
        functools.partial(unpack_kernel, groups),
        grid=(2,),
        in_specs=[
            pl.BlockSpec((heads, rows, PAIR), lambda t: (0, t, 0)),
            pl.BlockSpec((groups, heads, rows, PAIR), lambda t: (0, 0, t, 0)),
        ],
        out_specs=[flat] * 4,
        out_shape=[shape] * 4,
        name="unpack_heads",
    )(qa, kvg)


def body(queries, key_rows, value_rows, out_grad, dropout_bits, partner, block_pick, global_blocks):
    rows, cols = lax.axis_size("row"), lax.axis_size("col")
    qa, kvg = fused(
        rows, cols, queries, key_rows, value_rows, out_grad, dropout_bits, partner, block_pick, global_blocks
    )
    attended, query_grad, key_grad, value_grad = unpack(qa, kvg)
    return attended, query_grad, key_grad, value_grad


def solution(mesh):
    split = P(("row", "col"), None)
    return jax.shard_map(
        body,
        mesh=mesh,
        in_specs=(split,) * 5 + (P(),) * 3,
        out_specs=(split,) * 4,
        check_vma=False,
    )
```
